512 devices in a mesh: dp: 32 (over x, y, core), expert: 16 (over z).
Axes of the slice: x: 4, y: 4, z: 16, core: 2. Of those that a mesh axis runs over, the one named last changes fastest.
Arguments:
- tokens: bfloat16 [65536, 2048], P(('dp', 'expert')), may hold values from -200 to 200
- norm_gain: float32 [2048], replicated, may hold values from 0.1 to 1.9
- route_probs: float32 [65536, 8], P(('dp', 'expert')), may hold values from 0.02 to 4
- window_expert: int32 [65536], P(('dp', 'expert')), may hold values from 0 to 15, as said below
- w_gate_up: bfloat16 [16, 768, 4096], P('expert', 'dp'), may hold values from -0.125 to 0.125
- w_down: bfloat16 [16, 2048, 768], P('expert', 'dp'), may hold values from -0.21875 to 0.21875
Outputs:
- moe_out: bfloat16 [65536, 2048], P(('dp', 'expert'))
The draws below stay inside these ranges and needn't reach their ends.
Inputs may be any that keep to these rules, and one draw needn't show every extreme that they name: `window_expert`: in the tokens of one device no expert is named by more than 24 tokens; one expert, the same for every device, is named by exactly 24 tokens of every device.
All inputs are finite; a program needn't handle non-finite values.
Results may differ from the reference program's by a relative error of at most 0.0071.
Values may be sent and summed in bfloat16 or wider, within the bound.
No kernel may reach another device: no remote copies, remote signals or barrier semaphores. Data moves between devices by JAX's collectives and lax.ppermute only.
A program may use at most 64 MiB of HBM per device.

```python
import math
import jax
import jax.numpy as jnp
from jax import lax

D = 2048
FF = 768
TOP = 8
TOK_DEV = 128
NW = 16
CAP = 24
TOKENS = 65536
N_EXPERT = 16


def draw_window_expert(key, part):
    blocks = TOKENS // TOK_DEV
    hottest = jax.random.randint(jax.random.fold_in(key, 7), (), 0, N_EXPERT)
    lowest = (TOK_DEV - CAP + N_EXPERT - 2) // (N_EXPERT - 1)
    slots_all = N_EXPERT * CAP

    def one_block(block_key):
        key_caps, key_rank, key_spread = jax.random.split(block_key, 3)
        limits = jax.random.randint(key_caps, (N_EXPERT,), lowest, CAP + 1)
        limits = jnp.where(jnp.arange(N_EXPERT) == hottest, CAP, limits)
        label = jnp.arange(slots_all) // CAP
        within = jnp.arange(slots_all) % CAP
        usable = within < limits[label]
        ranking = jax.random.permutation(key_rank, slots_all)
        tier = jnp.where(label == hottest, 0, jnp.where(usable, 1, 2))
        score = tier * slots_all + ranking
        chosen = label[jnp.argsort(score, stable=True)[:TOK_DEV]]
        spread = jax.random.permutation(key_spread, TOK_DEV)
        return chosen[jnp.argsort(spread, stable=True)].astype(jnp.int32)
    block_keys = jax.random.split(jax.random.fold_in(key, 11), blocks)
    return jax.vmap(one_block)(block_keys).reshape(TOKENS).astype(jnp.int32)


def draw_tokens(key, part):
    key_base, key_rows, key_cols = jax.random.split(jax.random.fold_in(key, 3), 3)
    base = jnp.clip(jax.random.normal(key_base, (TOKENS, D), jnp.float32), -6.0, 6.0)
    rows = jnp.exp(jax.random.uniform(key_rows, (TOKENS, 1), jnp.float32, 0.0, math.log(10.0)))
    cols = jnp.exp(jax.random.uniform(key_cols, (1, D), jnp.float32, math.log(0.3), math.log(3.0)))
    return jnp.clip(base * rows * cols, -200.0, 200.0).astype(jnp.bfloat16)


def draw_route_probs(key, part):
    key_probs, key_lead = jax.random.split(jax.random.fold_in(key, 5), 2)
    probs = jnp.exp(jax.random.uniform(key_probs, (TOKENS, TOP), jnp.float32, math.log(0.02), 0.0))
    lead = jax.random.uniform(key_lead, (TOKENS, 1), jnp.float32, 1.0, 4.0)
    column = jnp.arange(TOP)[None, :]
    return jnp.where(column == 0, probs * lead, probs)


def level_of(rng, extent, cuts, least, high):
    def one(position, parts):
        draws = jax.random.uniform(jax.random.fold_in(jax.random.fold_in(rng, 6), position), (parts,), jnp.float32, least / len(cuts), high / len(cuts))
        return jnp.repeat(jnp.exp(draws), extent[position] // parts).reshape((-1,) + (1,) * (len(extent) - position - 1))

    level = one(*cuts[0])
    for cut in cuts[1:]:
        level = level * one(*cut)
    return level


def centred(stream_key, shape, scale, limit, cuts=(), kind=jnp.bfloat16):
    level = level_of(stream_key, shape, cuts, -0.22, 0.18) if cuts else 1.0
    values = jax.random.normal(stream_key, shape, jnp.float32) * scale * level
    return jnp.minimum(jnp.maximum(values, -limit), limit).astype(kind)


def setup_inputs(seed: int = 0) -> dict:
    arg_keys = jax.random.split(jax.random.key(seed), 7)
    tokens = draw_tokens(jax.random.fold_in(arg_keys[6], 71), 0)
    norm_gain = jnp.clip(1.0 + 0.18 * jax.random.normal(arg_keys[1], (D,), jnp.float32), 0.1, 1.9)
    route_probs = draw_route_probs(jax.random.fold_in(arg_keys[6], 71), 0)
    window_expert = draw_window_expert(jax.random.fold_in(arg_keys[6], 71), 0)
    w_gate_up = centred(arg_keys[4], (NW, FF, 2 * D), D ** -0.5, 0.125, ((0, 16), (1, 32)))
    w_down = centred(arg_keys[5], (NW, D, FF), FF ** -0.5, 0.21875, ((0, 16), (1, 32)))
    return dict(tokens=tokens, norm_gain=norm_gain, route_probs=route_probs, window_expert=window_expert, w_gate_up=w_gate_up, w_down=w_down)


row_block = 1024

def reference(tokens, norm_gain, route_probs, window_expert, w_gate_up, w_down):
    values = tokens.astype(jnp.float32)
    meansq = lax.optimization_barrier(jnp.mean(values * values, axis=1, keepdims=True))
    normed = (values * lax.rsqrt(meansq + 1e-06) * norm_gain[None, :]).astype(jnp.bfloat16)
    share = route_probs[:, 0] / lax.optimization_barrier(jnp.sum(route_probs, axis=1))
    order = jnp.argsort(window_expert, stable=True).astype(jnp.int32)
    sorted_rows = normed[order]
    padded = jnp.concatenate([sorted_rows, jnp.zeros((row_block, D), jnp.bfloat16)], axis=0)
    counts = lax.optimization_barrier(jnp.sum((window_expert[:, None] == jnp.arange(NW, dtype=jnp.int32)[None, :]).astype(jnp.int32), axis=0))
    starts = (jnp.cumsum(counts) - counts).astype(jnp.int32)
    result = jnp.zeros((TOKENS + row_block, D), jnp.float32)

    def per_expert(expert_id, res):
        first = starts[expert_id]
        count = counts[expert_id]
        both = w_gate_up[expert_id]
        down = w_down[expert_id]
        blocks = (count + row_block - 1) // row_block

        def per_block(index, acc):
            lower = (first + index * row_block).astype(jnp.int32)
            rows = lax.dynamic_slice_in_dim(padded, lower, row_block, 0)
            gate = lax.dot_general(rows, both[:, :D], (((1,), (1,)), ((), ())), preferred_element_type=jnp.float32)
            upper = lax.dot_general(rows, both[:, D:], (((1,), (1,)), ((), ())), preferred_element_type=jnp.float32)
            hidden = (jax.nn.silu(gate) * upper).astype(jnp.bfloat16)
            produced = lax.dot_general(hidden, down, (((1,), (1,)), ((), ())), preferred_element_type=jnp.float32)
            produced = produced.astype(jnp.bfloat16).astype(jnp.float32)
            live = (jnp.arange(row_block, dtype=jnp.int32) < count - index * row_block)[:, None]
            older = lax.dynamic_slice_in_dim(acc, lower, row_block, 0)
            return lax.dynamic_update_slice_in_dim(acc, older + jnp.where(live, produced, jnp.zeros_like(produced)), lower, 0)
        return lax.fori_loop(jnp.int32(0), blocks.astype(jnp.int32), per_block, res)
    result = lax.fori_loop(0, NW, per_expert, result)
    gathered = jnp.zeros((TOKENS, D), jnp.float32).at[order].set(result[:TOKENS])
    return (share[:, None] * gathered).astype(jnp.bfloat16)
```

```python
import jax
import jax.numpy as jnp
from jax import lax
from jax.sharding import PartitionSpec as P


def send_rows(outgoing):
    return lax.all_to_all(outgoing, "expert", split_axis=0, concat_axis=0, tiled=True)


def pack(both, down):
    corner = jnp.concatenate([down[48:56, 512:], down[56:64, 512:]], axis=1)
    tail = jnp.concatenate([down[48:64, :512], corner], axis=0)
    return jnp.concatenate([both, down[:24], down[24:48], tail], axis=1)


def unpack_down(gathered, width):
    rows = gathered[:, 2 * width :].reshape(-1, 24, width)
    third = jnp.concatenate(
        [
            rows[:, :16, 1536:],
            jnp.concatenate([rows[:, 16:, 1536:1792], rows[:, 16:, 1792:]], axis=1),
        ],
        axis=2,
    )
    down = jnp.concatenate([rows[:, :, :768], rows[:, :, 768:1536], third], axis=1)
    return down.reshape(width, 768)


def local(tokens, norm_gain, route_probs, window_expert, w_gate_up, w_down):
    tok_count = tokens.shape[0]
    width = tokens.shape[1]
    owners = lax.axis_size("expert")
    capacity = 3 * tok_count // owners
    values = tokens.astype(jnp.float32)
    meansq = jnp.mean(values * values, axis=1, keepdims=True)
    normed = (values * lax.rsqrt(meansq + 1e-06) * norm_gain[None, :]).astype(jnp.bfloat16)
    share = route_probs[:, 0] / jnp.sum(route_probs, axis=1)
    member = (window_expert[:, None] == jnp.arange(owners, dtype=jnp.int32)[None, :]).astype(
        jnp.int32
    )
    earlier = jnp.cumsum(member, axis=0) - member
    slot_index = jnp.sum(earlier * member, axis=1)
    place = window_expert * capacity + slot_index
    source = (
        jnp.full((owners * capacity,), tok_count, jnp.int32)
        .at[place]
        .set(jnp.arange(tok_count, dtype=jnp.int32))
    )
    outgoing = jnp.take(normed, source, axis=0, mode="fill", fill_value=0).reshape(
        owners, capacity, width
    )
    piece = lax.all_gather(pack(w_gate_up[0], w_down[0]), "dp", axis=0, tiled=True)
    down = unpack_down(piece, width)
    contract = (((1,), (1,)), ((), ()))
    arrived = send_rows(outgoing).reshape(owners * capacity, width)
    gate = lax.dot_general(arrived, piece[:, :width], contract, preferred_element_type=jnp.float32)
    upper = lax.dot_general(arrived, piece[:, width : 2 * width], contract, preferred_element_type=jnp.float32)
    hidden = (jax.nn.silu(gate) * upper).astype(jnp.bfloat16)
    produced = lax.dot_general(
        hidden,
        down,
        contract,
        preferred_element_type=jnp.float32,
    ).astype(jnp.bfloat16)
    returned = lax.all_to_all(
        produced.reshape(owners, capacity, width), "expert", split_axis=0, concat_axis=0, tiled=True
    )
    returned = returned.reshape(owners * capacity, width)
    picked = jnp.take(returned, place, axis=0).astype(jnp.float32)
    return (share[:, None] * picked).astype(jnp.bfloat16)


def solution(mesh):
    placed = (
        P(("dp", "expert"), None),
        P(),
        P(("dp", "expert"), None),
        P(("dp", "expert")),
        P("expert", "dp", None),
        P("expert", "dp", None),
    )
    return jax.shard_map(
        local, mesh=mesh, in_specs=placed, out_specs=P(("dp", "expert"), None), check_vma=False
    )
```

```python
import functools

import jax
import jax.numpy as jnp
from jax import lax
from jax.experimental import pallas as pl
from jax.experimental.pallas import tpu as pltpu
from jax.sharding import PartitionSpec as P

F32, BF16 = jnp.float32, jnp.bfloat16
NT = (((1,), (1,)), ((), ()))
NN = (((1,), (0,)), ((), ()))
REACH = 5
HOPS = tuple(h for d in range(1, REACH + 1) for h in (d, -d))
FAR = 7 - REACH
VMEM = pl.BlockSpec(memory_space=pltpu.VMEM)
HBM = pl.BlockSpec(memory_space=pltpu.HBM)


def shift(x, hops):
    ring = lax.axis_size("expert")
    return lax.ppermute(x, "expert", [(i, (i + hops) % ring) for i in range(ring)])


def trade(x, mask):
    return lax.ppermute(x, "dp", [(i, i ^ mask) for i in range(lax.axis_size("dp"))])


X_STEPS, Y_STEPS, CORE = (8, 24), (2, 6), 1


def gather(x, steps):
    for mask in steps[:-1]:
        x = jnp.concatenate([x, trade(x, mask)], axis=0)
    y = trade(x, steps[-1])
    return x, y, trade(x, CORE), trade(y, CORE)


def gray(k):
    return k ^ (k >> 1)


def place_mask(slot, x_first):
    low, high = gray(slot & 3), gray((slot >> 2) & 3)
    px, py = (low, high) if x_first else (high, low)
    return (px << 3) | (py << 1) | (slot >> 4)


def hidden_order(ff):
    k = jnp.arange(ff, dtype=jnp.int32)[:, None]
    low = jnp.where(k < 512, k & 15, 16 + (k & 7))
    mask = jnp.where(k < 512, place_mask(k >> 4, True), place_mask((k - 512) >> 3, False))
    unit = (mask ^ lax.axis_index("dp")) * 24 + low
    return (unit == jnp.arange(ff, dtype=jnp.int32)[None, :]).astype(BF16)


def pack_kernel(both_ref, down_ref, a_ref, b_ref):
    a_ref[0] = both_ref[:16]
    b_ref[0, :, :768] = down_ref[...]
    for j in range(8):
        b_ref[0, 8 * j : 8 * (j + 1), 768:] = both_ref[16:, 512 * j : 512 * (j + 1)]


def send_kernel(tok_ref, gain_ref, rel_ref, *outs, ring, cap):
    values = tok_ref[...].astype(F32)
    meansq = jnp.mean(values * values, axis=1, keepdims=True)
    normed = (values * lax.rsqrt(meansq + 1e-06) * gain_ref[...]).astype(BF16)
    rel = rel_ref[...]
    count = rel.shape[1]
    member = lax.broadcasted_iota(jnp.int32, (ring, count), 0) == rel
    before = lax.broadcasted_iota(jnp.int32, (count, count), 0) < lax.broadcasted_iota(
        jnp.int32, (count, count), 1
    )
    earlier = lax.dot_general(
        member.astype(F32), before.astype(F32), NN, preferred_element_type=F32
    )
    slot = jnp.sum(jnp.where(member, earlier, 0.0), axis=0, keepdims=True).astype(jnp.int32)
    place = rel * cap + slot
    pick = lax.broadcasted_iota(jnp.int32, (ring * cap, count), 0) == place
    rows = lax.dot_general(
        pick.astype(F32).astype(BF16), normed, NN, preferred_element_type=F32
    )
    for hops, out in zip((0,) + HOPS, outs):
        own = (hops % ring) * cap
        out[0] = rows[own : own + cap].astype(BF16)
        if abs(hops) <= FAR:
            other = ((hops + ring // 2) % ring) * cap
            out[1] = rows[other : other + cap].astype(BF16)


def expert_kernel(x_ref, order_ref, *rest, cap):
    pieces_a, pieces_b = rest[:4], rest[4:8]
    outs, (wa, wb, wd, hid, sem_a, sem_b, sem_d) = rest[8:-7], rest[-7:]
    width = x_ref.shape[1]
    me = lax.axis_index("dp")
    each = pieces_a[0].shape[0]
    copies_a = [
        pltpu.make_async_copy(piece, wa.at[pl.ds(each * q, each)], sem_a.at[q])
        for q, piece in enumerate(pieces_a)
    ]
    copies_b, copies_d = [], []
    for q, piece in enumerate(pieces_b):
        for j in range(8):
            copies_b.append(
                pltpu.make_async_copy(
                    piece.at[:, pl.ds(8 * j, 8), pl.ds(768, 512)],
                    wb.at[pl.ds(each * q, each), :, pl.ds(512 * j, 512)],
                    sem_b.at[8 * q + j],
                )
            )
        for p in range(each):
            slot = each * q + p
            copies_d.append(
                pltpu.make_async_copy(
                    piece.at[p, :, pl.ds(0, 768)],
                    wd.at[me ^ place_mask(slot, False)],
                    sem_d.at[slot],
                )
            )
    for copy in copies_a + copies_b + copies_d:
        copy.start()
    x = x_ref[...]

    def units(w, cols):
        gate = lax.dot_general(x, w[:, :width], NT, preferred_element_type=F32)
        upper = lax.dot_general(x, w[:, width:], NT, preferred_element_type=F32)
        hid[:, cols] = (gate / (1.0 + jnp.exp(-gate)) * upper).astype(BF16)

    half = 2 * each * 16
    for c in range(2):
        copies_a[2 * c].wait()
        copies_a[2 * c + 1].wait()
        units(wa[2 * each * c : 2 * each * (c + 1)].reshape(half, 2 * width), slice(half * c, half * (c + 1)))
    for copy in copies_b:
        copy.wait()
    units(wb[...].reshape(256, 2 * width), slice(2 * half, 2 * half + 256))
    hidden = lax.dot_general(hid[...], order_ref[...], NN, preferred_element_type=F32).astype(BF16)
    for copy in copies_d:
        copy.wait()
    shards, feats, ff = wd.shape
    group = 8
    for n in range(shards // group):
        down = wd[group * n : group * (n + 1)].reshape(group * feats, ff)
        made = lax.dot_general(hidden, down, NT, preferred_element_type=F32)
        cols = slice(group * feats * n, group * feats * (n + 1))
        for b, out in enumerate(outs):
            out[:, cols] = made[cap * b : cap * (b + 1)].astype(BF16)


def run_expert(x, order, pieces_a, pieces_b, cap):
    rows, width = x.shape
    blocks = rows // cap
    ff = order.shape[0]
    shards = 4 * pieces_a[0].shape[0]
    return pl.pallas_call(
        functools.partial(expert_kernel, cap=cap),
        out_shape=[jax.ShapeDtypeStruct((cap, width), BF16)] * blocks,
        in_specs=[VMEM, VMEM] + [HBM] * 8,
        out_specs=[VMEM] * blocks,
        scratch_shapes=[
            pltpu.VMEM((shards, 16, 2 * width), BF16),
            pltpu.VMEM((shards, 8, 2 * width), BF16),
            pltpu.VMEM((shards, width // shards, ff), BF16),
            pltpu.VMEM((rows, ff), BF16),
            pltpu.SemaphoreType.DMA((4,)),
            pltpu.SemaphoreType.DMA((32,)),
            pltpu.SemaphoreType.DMA((32,)),
        ],
        compiler_params=pltpu.CompilerParams(vmem_limit_bytes=55 << 20),
        cost_estimate=pl.CostEstimate(
            flops=6 * rows * width * ff,
            bytes_accessed=6 * width * ff + 4 * x.size,
            transcendentals=rows * ff,
        ),
        name="expert",
    )(x, order, *pieces_a, *pieces_b)


def picks(rel, ring, cap, own):
    count = rel.shape[0]
    member = lax.broadcasted_iota(jnp.int32, (count, ring), 1) == rel
    before = lax.broadcasted_iota(jnp.int32, (count, count), 1) < lax.broadcasted_iota(
        jnp.int32, (count, count), 0
    )
    earlier = lax.dot_general(
        before.astype(F32), member.astype(F32), NN, preferred_element_type=F32
    )
    slot = jnp.sum(jnp.where(member, earlier, 0.0), axis=1, keepdims=True).astype(jnp.int32)
    half = ring // 2
    near = jnp.where(rel >= half, rel - ring, rel) if own else rel - half
    reach = REACH if own else FAR
    block = jnp.where(near > 0, 2 * near - 1, -2 * near)
    inside = jnp.abs(near) <= reach
    place = jnp.where(inside, block * cap + slot, -1)
    blocks = 2 * reach + 1
    cols = lax.broadcasted_iota(jnp.int32, (count, blocks * cap), 1)
    return (cols == place).astype(F32).astype(BF16)


def own_kernel(rel_ref, x_ref, out_ref, *, ring, cap):
    pick = picks(rel_ref[...], ring, cap, True)
    out_ref[...] = lax.dot_general(pick, x_ref[...], NN, preferred_element_type=F32).astype(BF16)


def last_kernel(rel_ref, probs_ref, part_ref, x_ref, out_ref, *, ring, cap):
    pick = picks(rel_ref[...], ring, cap, False)
    probs = probs_ref[...]
    share = probs[:, :1] / jnp.sum(probs, axis=1, keepdims=True)
    got = lax.dot_general(pick, x_ref[...], NN, preferred_element_type=F32)
    out_ref[...] = (share * (part_ref[...].astype(F32) + got)).astype(BF16)


def local(tokens, norm_gain, route_probs, window_expert, w_gate_up, w_down):
    tok_count, width = tokens.shape
    ring = lax.axis_size("expert")
    cap = 3 * tok_count // ring
    ff = w_down.shape[2]
    mine_a, mine_b = pl.pallas_call(
        pack_kernel,
        out_shape=[
            jax.ShapeDtypeStruct((1, 16, 2 * width), BF16),
            jax.ShapeDtypeStruct((1, 64, 1280), BF16),
        ],
        in_specs=[VMEM] * 2,
        out_specs=[VMEM] * 2,
        name="pack",
    )(w_gate_up[0], w_down[0])
    theirs_a, theirs_b = shift(mine_a, ring // 2), shift(mine_b, ring // 2)
    own_w = gather(mine_a, X_STEPS + Y_STEPS), gather(mine_b, Y_STEPS + X_STEPS)
    other_w = gather(theirs_a, X_STEPS + Y_STEPS), gather(theirs_b, Y_STEPS + X_STEPS)
    order = hidden_order(ff)

    rel = lax.rem(window_expert - lax.axis_index("expert") + ring, ring)
    sent = pl.pallas_call(
        functools.partial(send_kernel, ring=ring, cap=cap),
        out_shape=[
            jax.ShapeDtypeStruct((2 if abs(h) <= FAR else 1, cap, width), BF16) for h in (0,) + HOPS
        ],
        in_specs=[VMEM] * 3,
        out_specs=[VMEM] * (1 + len(HOPS)),
        compiler_params=pltpu.CompilerParams(vmem_limit_bytes=28 << 20),
        cost_estimate=pl.CostEstimate(
            flops=6 * tok_count * tok_count * width,
            bytes_accessed=8 * tokens.size,
            transcendentals=0,
        ),
        name="send",
    )(tokens, norm_gain[None, :], rel[None, :])
    got = [sent[0]] + [shift(x, h) for h, x in zip(HOPS, sent[1:])]
    own_x = jnp.concatenate([x[0] for x in got], axis=0)
    other_x = jnp.concatenate([x[1] for x in got[: 1 + 2 * FAR]], axis=0)

    def back(ys):
        return jnp.concatenate([ys[0]] + [shift(y, -h) for h, y in zip(HOPS, ys[1:])], axis=0)

    own_back = back(run_expert(own_x, order, *own_w, cap))
    rel_col = rel[:, None]
    pick_cost = pl.CostEstimate(
        flops=4 * tok_count * tok_count * width, bytes_accessed=8 * tokens.size, transcendentals=0
    )
    part = pl.pallas_call(
        functools.partial(own_kernel, ring=ring, cap=cap),
        out_shape=jax.ShapeDtypeStruct((tok_count, width), BF16),
        in_specs=[VMEM] * 2,
        out_specs=VMEM,
        cost_estimate=pick_cost,
        compiler_params=pltpu.CompilerParams(vmem_limit_bytes=12 << 20),
        name="own_back",
    )(rel_col, own_back)

    other_back = back(run_expert(other_x, order, *other_w, cap))
    return pl.pallas_call(
        functools.partial(last_kernel, ring=ring, cap=cap),
        out_shape=jax.ShapeDtypeStruct((tok_count, width), BF16),
        in_specs=[VMEM] * 4,
        out_specs=VMEM,
        cost_estimate=pick_cost,
        compiler_params=pltpu.CompilerParams(vmem_limit_bytes=12 << 20),
        name="last",
    )(rel_col, route_probs, part, other_back)


def solution(mesh):
    placed = (
        P(("dp", "expert"), None),
        P(),
        P(("dp", "expert"), None),
        P(("dp", "expert")),
        P("expert", "dp", None),
        P("expert", "dp", None),
    )
    return jax.shard_map(
        local, mesh=mesh, in_specs=placed, out_specs=P(("dp", "expert"), None), check_vma=False
    )
```

```python
import functools

import jax
import jax.numpy as jnp
from jax import lax
from jax.experimental import pallas as pl
from jax.experimental.pallas import tpu as pltpu
from jax.sharding import PartitionSpec as P

F32, BF16 = jnp.float32, jnp.bfloat16
NT = (((1,), (1,)), ((), ()))
NN = (((1,), (0,)), ((), ()))
VMEM = pl.BlockSpec(memory_space=pltpu.VMEM)
HBM = pl.BlockSpec(memory_space=pltpu.HBM)
ANY = pl.BlockSpec(memory_space=pl.ANY)


def trade(x, mask):
    return lax.ppermute(x, "dp", [(i, i ^ mask) for i in range(lax.axis_size("dp"))])


X_STEPS, Y_STEPS, CORE = (8, 24), (2, 6), 1


def gather(x, steps):
    for mask in steps[:-1]:
        x = jnp.concatenate([x, trade(x, mask)], axis=0)
    y = trade(x, steps[-1])
    return x, y, trade(x, CORE), trade(y, CORE)


def gray(k):
    return k ^ (k >> 1)


def place_mask(slot, x_first):
    low, high = gray(slot & 3), gray((slot >> 2) & 3)
    px, py = (low, high) if x_first else (high, low)
    return (px << 3) | (py << 1) | (slot >> 4)


def send_kernel(tok_ref, gain_ref, expert_ref, out_ref, *, ring, cap):
    values = tok_ref[...].astype(F32)
    meansq = jnp.mean(values * values, axis=1, keepdims=True)
    normed = (values * lax.rsqrt(meansq + 1e-06) * gain_ref[...]).astype(BF16)
    expert = expert_ref[...]
    count = expert.shape[1]
    member = lax.broadcasted_iota(jnp.int32, (ring, count), 0) == expert
    before = lax.broadcasted_iota(jnp.int32, (count, count), 0) < lax.broadcasted_iota(
        jnp.int32, (count, count), 1
    )
    earlier = lax.dot_general(
        member.astype(F32), before.astype(F32), NN, preferred_element_type=F32
    )
    slot = jnp.sum(jnp.where(member, earlier, 0.0), axis=0, keepdims=True).astype(jnp.int32)
    place = expert * cap + slot
    pick = lax.broadcasted_iota(jnp.int32, (ring * cap, count), 0) == place
    out_ref[...] = lax.dot_general(
        pick.astype(F32).astype(BF16), normed, NN, preferred_element_type=F32
    ).astype(BF16)


def arrange_kernel(*refs):
    pieces_a, pieces_b, (up, down, sem_a, sem_b) = refs[:4], refs[4:8], refs[8:]
    me = lax.axis_index("dp")
    each = pieces_a[0].shape[0]
    copies = []
    for q in range(4):
        for p in range(each):
            slot = each * q + p
            for pieces, whole, sem, x_first in (
                (pieces_a, up, sem_a, True),
                (pieces_b, down, sem_b, False),
            ):
                copies.append(
                    pltpu.make_async_copy(
                        pieces[q].at[p], whole.at[me ^ place_mask(slot, x_first)], sem.at[slot]
                    )
                )
    for copy in copies:
        copy.start()
    for copy in copies:
        copy.wait()


def arrange(pieces_a, pieces_b):
    shapes = [(4 * ps[0].shape[0],) + ps[0].shape[1:] for ps in (pieces_a, pieces_b)]
    return pl.pallas_call(
        arrange_kernel,
        out_shape=[jax.ShapeDtypeStruct(shape, BF16) for shape in shapes],
        in_specs=[ANY] * 8,
        out_specs=[HBM] * 2,
        scratch_shapes=[pltpu.SemaphoreType.DMA((shapes[0][0],))] * 2,
        cost_estimate=pl.CostEstimate(flops=0, bytes_accessed=38 << 19, transcendentals=0),
        name="arrange",
    )(*pieces_a, *pieces_b)


def expert_kernel(x_ref, up_hbm, down_hbm, out_ref, up_ref, down_ref, hid, sem_up, sem_down):
    width, ff = x_ref.shape[1], hid.shape[1]
    parts_up, parts_down = sem_up.shape[0], sem_down.shape[0]
    ups = [slice(c * ff // parts_up, (c + 1) * ff // parts_up) for c in range(parts_up)]
    downs = [slice(c * width // parts_down, (c + 1) * width // parts_down) for c in range(parts_down)]
    copies_up = [
        pltpu.make_async_copy(up_hbm.at[part], up_ref.at[part], sem_up.at[c])
        for c, part in enumerate(ups)
    ]
    copies_down = [
        pltpu.make_async_copy(down_hbm.at[part], down_ref.at[part], sem_down.at[c])
        for c, part in enumerate(downs)
    ]
    for copy in copies_up + copies_down:
        copy.start()
    x = x_ref[...]
    for copy, part in zip(copies_up, ups):
        copy.wait()
        gate = lax.dot_general(x, up_ref[part, :width], NT, preferred_element_type=F32)
        upper = lax.dot_general(x, up_ref[part, width:], NT, preferred_element_type=F32)
        hid[:, part] = (gate / (1.0 + jnp.exp(-gate)) * upper).astype(BF16)
    hidden = hid[...]
    for copy, part in zip(copies_down, downs):
        copy.wait()
        out_ref[:, part] = lax.dot_general(
            hidden, down_ref[part], NT, preferred_element_type=F32
        ).astype(BF16)


def last_kernel(expert_ref, probs_ref, x_ref, out_ref, *, ring, cap):
    expert = expert_ref[...]
    count = expert.shape[0]
    member = lax.broadcasted_iota(jnp.int32, (count, ring), 1) == expert
    before = lax.broadcasted_iota(jnp.int32, (count, count), 1) < lax.broadcasted_iota(
        jnp.int32, (count, count), 0
    )
    earlier = lax.dot_general(
        before.astype(F32), member.astype(F32), NN, preferred_element_type=F32
    )
    slot = jnp.sum(jnp.where(member, earlier, 0.0), axis=1, keepdims=True).astype(jnp.int32)
    place = expert * cap + slot
    pick = lax.broadcasted_iota(jnp.int32, (count, ring * cap), 1) == place
    probs = probs_ref[...]
    share = probs[:, :1] / jnp.sum(probs, axis=1, keepdims=True)
    got = lax.dot_general(
        pick.astype(F32).astype(BF16), x_ref[...], NN, preferred_element_type=F32
    )
    out_ref[...] = (share * got).astype(BF16)


def exchange(x, ring):
    blocks = x.reshape(ring, x.shape[0] // ring, x.shape[1])
    return lax.all_to_all(blocks, "expert", split_axis=0, concat_axis=0, tiled=True).reshape(x.shape)


def local(tokens, norm_gain, route_probs, window_expert, w_gate_up, w_down):
    tok_count, width = tokens.shape
    ring = lax.axis_size("expert")
    cap = 3 * tok_count // ring
    rows = ring * cap
    ff = w_down.shape[2]
    sent = pl.pallas_call(
        functools.partial(send_kernel, ring=ring, cap=cap),
        out_shape=jax.ShapeDtypeStruct((rows, width), BF16),
        in_specs=[VMEM] * 3,
        out_specs=VMEM,
        compiler_params=pltpu.CompilerParams(vmem_limit_bytes=20 << 20),
        cost_estimate=pl.CostEstimate(
            flops=6 * tok_count * tok_count * width,
            bytes_accessed=8 * tokens.size,
            transcendentals=0,
        ),
        name="send",
    )(tokens, norm_gain[None, :], window_expert[None, :])
    x = exchange(sent, ring)
    up, down = arrange(gather(w_gate_up, X_STEPS + Y_STEPS), gather(w_down, Y_STEPS + X_STEPS))
    made = pl.pallas_call(
        expert_kernel,
        out_shape=jax.ShapeDtypeStruct((rows, width), BF16),
        in_specs=[VMEM, HBM, HBM],
        out_specs=VMEM,
        scratch_shapes=[
            pltpu.VMEM((ff, 2 * width), BF16),
            pltpu.VMEM((width, ff), BF16),
            pltpu.VMEM((rows, ff), BF16),
            pltpu.SemaphoreType.DMA((3,)),
            pltpu.SemaphoreType.DMA((4,)),
        ],
        compiler_params=pltpu.CompilerParams(vmem_limit_bytes=55 << 20),
        cost_estimate=pl.CostEstimate(
            flops=6 * rows * width * ff,
            bytes_accessed=6 * width * ff + 4 * x.size,
            transcendentals=rows * ff,
        ),
        name="expert",
    )(x, up.reshape(ff, 2 * width), down.reshape(width, ff))
    return pl.pallas_call(
        functools.partial(last_kernel, ring=ring, cap=cap),
        out_shape=jax.ShapeDtypeStruct((tok_count, width), BF16),
        in_specs=[VMEM] * 3,
        out_specs=VMEM,
        cost_estimate=pl.CostEstimate(
            flops=6 * tok_count * tok_count * width, bytes_accessed=8 * tokens.size, transcendentals=0
        ),
        compiler_params=pltpu.CompilerParams(vmem_limit_bytes=16 << 20),
        name="last",
    )(window_expert[:, None], route_probs, exchange(made, ring))


def solution(mesh):
    placed = (
        P(("dp", "expert"), None),
        P(),
        P(("dp", "expert"), None),
        P(("dp", "expert")),
        P("expert", "dp", None),
        P("expert", "dp", None),
    )
    return jax.shard_map(
        local, mesh=mesh, in_specs=placed, out_specs=P(("dp", "expert"), None), check_vma=False
    )
```

```python
import functools

import jax
import jax.numpy as jnp
from jax import lax
from jax.experimental import pallas as pl
from jax.experimental.pallas import tpu as pltpu
from jax.sharding import PartitionSpec as P

F32, BF16 = jnp.float32, jnp.bfloat16
NT = (((1,), (1,)), ((), ()))
NN = (((1,), (0,)), ((), ()))
VMEM = pl.BlockSpec(memory_space=pltpu.VMEM)
HBM = pl.BlockSpec(memory_space=pltpu.HBM)
ANY = pl.BlockSpec(memory_space=pl.ANY)


def trade(x, mask):
    return lax.ppermute(x, "dp", [(i, i ^ mask) for i in range(lax.axis_size("dp"))])


X_STEPS, Y_STEPS, CORE = (8, 24), (2, 6), 1


def gather(a, b):
    a_steps, b_steps = X_STEPS + Y_STEPS, Y_STEPS + X_STEPS
    for a_mask, b_mask in zip(a_steps[:-1], b_steps[:-1]):
        a_in, b_in = lax.optimization_barrier((trade(a, a_mask), trade(b, b_mask)))
        a, b = jnp.concatenate([a, a_in], axis=0), jnp.concatenate([b, b_in], axis=0)
    a_in, b_in, a_near, b_near = lax.optimization_barrier(
        (trade(a, a_steps[-1]), trade(b, b_steps[-1]), trade(a, CORE), trade(b, CORE))
    )
    return (a, a_in, a_near, trade(a_in, CORE)), (b, b_in, b_near, trade(b_in, CORE))


def gray(k):
    return k ^ (k >> 1)


def place_mask(slot, x_first):
    low, high = gray(slot & 3), gray((slot >> 2) & 3)
    px, py = (low, high) if x_first else (high, low)
    return (px << 3) | (py << 1) | (slot >> 4)


def send_kernel(tok_ref, gain_ref, expert_ref, out_ref, *, ring, cap):
    values = tok_ref[...].astype(F32)
    meansq = jnp.mean(values * values, axis=1, keepdims=True)
    normed = (values * lax.rsqrt(meansq + 1e-06) * gain_ref[...]).astype(BF16)
    expert = expert_ref[...]
    count = expert.shape[1]
    member = lax.broadcasted_iota(jnp.int32, (ring, count), 0) == expert
    before = lax.broadcasted_iota(jnp.int32, (count, count), 0) < lax.broadcasted_iota(
        jnp.int32, (count, count), 1
    )
    earlier = lax.dot_general(
        member.astype(F32), before.astype(F32), NN, preferred_element_type=F32
    )
    slot = jnp.sum(jnp.where(member, earlier, 0.0), axis=0, keepdims=True).astype(jnp.int32)
    place = expert * cap + slot
    pick = lax.broadcasted_iota(jnp.int32, (ring * cap, count), 0) == place
    out_ref[...] = lax.dot_general(
        pick.astype(F32).astype(BF16), normed, NN, preferred_element_type=F32
    ).astype(BF16)


def arrange_kernel(*refs):
    pieces_a, pieces_b, (up, down, sem_a, sem_b) = refs[:4], refs[4:8], refs[8:]
    me = lax.axis_index("dp")
    each = pieces_a[0].shape[0]
    copies = []
    for q in range(4):
        for p in range(each):
            slot = each * q + p
            for pieces, whole, sem, x_first in (
                (pieces_a, up, sem_a, True),
                (pieces_b, down, sem_b, False),
            ):
                copies.append(
                    pltpu.make_async_copy(
                        pieces[q].at[p], whole.at[me ^ place_mask(slot, x_first)], sem.at[slot]
                    )
                )
    for copy in copies:
        copy.start()
    for copy in copies:
        copy.wait()


def arrange(pieces_a, pieces_b):
    shapes = [(4 * ps[0].shape[0],) + ps[0].shape[1:] for ps in (pieces_a, pieces_b)]
    return pl.pallas_call(
        arrange_kernel,
        out_shape=[jax.ShapeDtypeStruct(shape, BF16) for shape in shapes],
        in_specs=[ANY] * 8,
        out_specs=[VMEM] * 2,
        compiler_params=pltpu.CompilerParams(vmem_limit_bytes=20 << 20),
        scratch_shapes=[pltpu.SemaphoreType.DMA((shapes[0][0],))] * 2,
        cost_estimate=pl.CostEstimate(flops=0, bytes_accessed=38 << 19, transcendentals=0),
        name="arrange",
    )(*pieces_a, *pieces_b)


def expert_kernel(x_ref, up_hbm, down_hbm, out_ref, up_ref, down_ref, hid, sem_up, sem_down):
    width, ff = x_ref.shape[1], hid.shape[1]
    parts_up, parts_down = sem_up.shape[0], sem_down.shape[0]
    ups = [slice(c * ff // parts_up, (c + 1) * ff // parts_up) for c in range(parts_up)]
    downs = [slice(c * width // parts_down, (c + 1) * width // parts_down) for c in range(parts_down)]
    copies_up = [
        pltpu.make_async_copy(up_hbm.at[part], up_ref.at[part], sem_up.at[c])
        for c, part in enumerate(ups)
    ]
    copies_down = [
        pltpu.make_async_copy(down_hbm.at[part], down_ref.at[part], sem_down.at[c])
        for c, part in enumerate(downs)
    ]
    for copy in copies_up + copies_down:
        copy.start()
    x = x_ref[...]
    for copy, part in zip(copies_up, ups):
        copy.wait()
        gate = lax.dot_general(x, up_ref[part, :width], NT, preferred_element_type=F32)
        upper = lax.dot_general(x, up_ref[part, width:], NT, preferred_element_type=F32)
        hid[:, part] = (gate / (1.0 + jnp.exp(-gate)) * upper).astype(BF16)
    hidden = hid[...]
    for copy, part in zip(copies_down, downs):
        copy.wait()
        out_ref[:, part] = lax.dot_general(
            hidden, down_ref[part], NT, preferred_element_type=F32
        ).astype(BF16)


def last_kernel(expert_ref, probs_ref, x_ref, out_ref, *, ring, cap):
    expert = expert_ref[...]
    count = expert.shape[0]
    member = lax.broadcasted_iota(jnp.int32, (count, ring), 1) == expert
    before = lax.broadcasted_iota(jnp.int32, (count, count), 1) < lax.broadcasted_iota(
        jnp.int32, (count, count), 0
    )
    earlier = lax.dot_general(
        before.astype(F32), member.astype(F32), NN, preferred_element_type=F32
    )
    slot = jnp.sum(jnp.where(member, earlier, 0.0), axis=1, keepdims=True).astype(jnp.int32)
    place = expert * cap + slot
    pick = lax.broadcasted_iota(jnp.int32, (count, ring * cap), 1) == place
    probs = probs_ref[...]
    share = probs[:, :1] / jnp.sum(probs, axis=1, keepdims=True)
    got = lax.dot_general(
        pick.astype(F32).astype(BF16), x_ref[...], NN, preferred_element_type=F32
    )
    out_ref[...] = (share * got).astype(BF16)


def exchange(x, ring):
    blocks = x.reshape(ring, x.shape[0] // ring, x.shape[1])
    return lax.all_to_all(blocks, "expert", split_axis=0, concat_axis=0, tiled=True).reshape(x.shape)


def local(tokens, norm_gain, route_probs, window_expert, w_gate_up, w_down):
    tok_count, width = tokens.shape
    ring = lax.axis_size("expert")
    cap = 3 * tok_count // ring
    rows = ring * cap
    ff = w_down.shape[2]
    sent = pl.pallas_call(
        functools.partial(send_kernel, ring=ring, cap=cap),
        out_shape=jax.ShapeDtypeStruct((rows, width), BF16),
        in_specs=[VMEM] * 3,
        out_specs=VMEM,
        compiler_params=pltpu.CompilerParams(vmem_limit_bytes=20 << 20),
        cost_estimate=pl.CostEstimate(
            flops=6 * tok_count * tok_count * width,
            bytes_accessed=8 * tokens.size,
            transcendentals=0,
        ),
        name="send",
    )(tokens, norm_gain[None, :], window_expert[None, :])
    x = exchange(sent, ring)
    up, down = arrange(*gather(w_gate_up, w_down))
    made = pl.pallas_call(
        expert_kernel,
        out_shape=jax.ShapeDtypeStruct((rows, width), BF16),
        in_specs=[VMEM, HBM, HBM],
        out_specs=VMEM,
        scratch_shapes=[
            pltpu.VMEM((ff, 2 * width), BF16),
            pltpu.VMEM((width, ff), BF16),
            pltpu.VMEM((rows, ff), BF16),
            pltpu.SemaphoreType.DMA((3,)),
            pltpu.SemaphoreType.DMA((4,)),
        ],
        compiler_params=pltpu.CompilerParams(vmem_limit_bytes=55 << 20),
        cost_estimate=pl.CostEstimate(
            flops=6 * rows * width * ff,
            bytes_accessed=6 * width * ff + 4 * x.size,
            transcendentals=rows * ff,
        ),
        name="expert",
    )(x, up.reshape(ff, 2 * width), down.reshape(width, ff))
    return pl.pallas_call(
        functools.partial(last_kernel, ring=ring, cap=cap),
        out_shape=jax.ShapeDtypeStruct((tok_count, width), BF16),
        in_specs=[VMEM] * 3,
        out_specs=VMEM,
        cost_estimate=pl.CostEstimate(
            flops=6 * tok_count * tok_count * width, bytes_accessed=8 * tokens.size, transcendentals=0
        ),
        compiler_params=pltpu.CompilerParams(vmem_limit_bytes=16 << 20),
        name="last",
    )(window_expert[:, None], route_probs, exchange(made, ring))


def solution(mesh):
    placed = (
        P(("dp", "expert"), None),
        P(),
        P(("dp", "expert"), None),
        P(("dp", "expert")),
        P("expert", "dp", None),
        P("expert", "dp", None),
    )
    return jax.shard_map(
        local, mesh=mesh, in_specs=placed, out_specs=P(("dp", "expert"), None), check_vma=False
    )
```

```python
import functools

import jax
import jax.numpy as jnp
from jax import lax
from jax.experimental import pallas as pl
from jax.experimental.pallas import tpu as pltpu
from jax.sharding import PartitionSpec as P

F32, BF16 = jnp.float32, jnp.bfloat16
NT = (((1,), (1,)), ((), ()))
NN = (((1,), (0,)), ((), ()))
VMEM = pl.BlockSpec(memory_space=pltpu.VMEM)
HBM = pl.BlockSpec(memory_space=pltpu.HBM)
ANY = pl.BlockSpec(memory_space=pl.ANY)


def trade(x, mask):
    return lax.ppermute(x, "dp", [(i, i ^ mask) for i in range(lax.axis_size("dp"))])


X_STEPS, Y_STEPS, CORE = (8, 24), (2, 6), 1


def gather(a, b):
    a_steps, b_steps = X_STEPS + Y_STEPS, Y_STEPS + X_STEPS
    for a_mask, b_mask in zip(a_steps[:-1], b_steps[:-1]):
        a_in, b_in = lax.optimization_barrier((trade(a, a_mask), trade(b, b_mask)))
        a, b = jnp.concatenate([a, a_in], axis=0), jnp.concatenate([b, b_in], axis=0)
    a_in, b_in, a_near, b_near = lax.optimization_barrier(
        (trade(a, a_steps[-1]), trade(b, b_steps[-1]), trade(a, CORE), trade(b, CORE))
    )
    return (a, a_in, a_near, trade(a_in, CORE)), (b, b_in, b_near, trade(b_in, CORE))


def gray(k):
    return k ^ (k >> 1)


def place_mask(slot, x_first):
    low, high = gray(slot & 3), gray((slot >> 2) & 3)
    px, py = (low, high) if x_first else (high, low)
    return (px << 3) | (py << 1) | (slot >> 4)


def hidden_order(ff):
    k = jnp.arange(ff, dtype=jnp.int32)[:, None]
    low = jnp.where(k < 512, k & 15, 16 + (k & 7))
    mask = jnp.where(k < 512, place_mask(k >> 4, True), place_mask((k - 512) >> 3, False))
    unit = (mask ^ lax.axis_index("dp")) * 24 + low
    return (unit == jnp.arange(ff, dtype=jnp.int32)[None, :]).astype(BF16)


def pack_kernel(both_ref, down_ref, a_ref, b_ref):
    a_ref[0] = both_ref[:16]
    b_ref[0, :, :768] = down_ref[...]
    for j in range(8):
        b_ref[0, 8 * j : 8 * (j + 1), 768:] = both_ref[16:, 512 * j : 512 * (j + 1)]


def send_kernel(tok_ref, gain_ref, expert_ref, out_ref, *, ring, cap):
    values = tok_ref[...].astype(F32)
    meansq = jnp.mean(values * values, axis=1, keepdims=True)
    normed = (values * lax.rsqrt(meansq + 1e-06) * gain_ref[...]).astype(BF16)
    expert = expert_ref[...]
    count = expert.shape[1]
    member = lax.broadcasted_iota(jnp.int32, (ring, count), 0) == expert
    before = lax.broadcasted_iota(jnp.int32, (count, count), 0) < lax.broadcasted_iota(
        jnp.int32, (count, count), 1
    )
    earlier = lax.dot_general(
        member.astype(F32), before.astype(F32), NN, preferred_element_type=F32
    )
    slot = jnp.sum(jnp.where(member, earlier, 0.0), axis=0, keepdims=True).astype(jnp.int32)
    place = expert * cap + slot
    pick = lax.broadcasted_iota(jnp.int32, (ring * cap, count), 0) == place
    out_ref[...] = lax.dot_general(
        pick.astype(F32).astype(BF16), normed, NN, preferred_element_type=F32
    ).astype(BF16)


def expert_kernel(x_ref, order_ref, *rest):
    pieces_a, pieces_b = rest[:4], rest[4:8]
    out_ref, wa, wb, wd, hid, sem_a, sem_b, sem_d = rest[8:]
    width = x_ref.shape[1]
    me = lax.axis_index("dp")
    each = pieces_a[0].shape[0]
    copies_a = [
        pltpu.make_async_copy(piece, wa.at[pl.ds(each * q, each)], sem_a.at[q])
        for q, piece in enumerate(pieces_a)
    ]
    copies_b, copies_d = [], []
    for q, piece in enumerate(pieces_b):
        for j in range(8):
            copies_b.append(
                pltpu.make_async_copy(
                    piece.at[:, pl.ds(8 * j, 8), pl.ds(768, 512)],
                    wb.at[pl.ds(each * q, each), :, pl.ds(512 * j, 512)],
                    sem_b.at[8 * q + j],
                )
            )
        for p in range(each):
            slot = each * q + p
            copies_d.append(
                pltpu.make_async_copy(
                    piece.at[p, :, pl.ds(0, 768)],
                    wd.at[me ^ place_mask(slot, False)],
                    sem_d.at[slot],
                )
            )
    for copy in copies_a + copies_b + copies_d:
        copy.start()
    x = x_ref[...]

    def units(w, cols):
        gate = lax.dot_general(x, w[:, :width], NT, preferred_element_type=F32)
        upper = lax.dot_general(x, w[:, width:], NT, preferred_element_type=F32)
        hid[:, cols] = (gate / (1.0 + jnp.exp(-gate)) * upper).astype(BF16)

    half = 2 * each * 16
    for c in range(2):
        copies_a[2 * c].wait()
        copies_a[2 * c + 1].wait()
        units(wa[2 * each * c : 2 * each * (c + 1)].reshape(half, 2 * width), slice(half * c, half * (c + 1)))
    for copy in copies_b:
        copy.wait()
    units(wb[...].reshape(256, 2 * width), slice(2 * half, 2 * half + 256))
    hidden = lax.dot_general(hid[...], order_ref[...], NN, preferred_element_type=F32).astype(BF16)
    for copy in copies_d:
        copy.wait()
    shards, feats, ff = wd.shape
    group = 8
    for n in range(shards // group):
        down = wd[group * n : group * (n + 1)].reshape(group * feats, ff)
        made = lax.dot_general(hidden, down, NT, preferred_element_type=F32)
        cols = slice(group * feats * n, group * feats * (n + 1))
        out_ref[:, cols] = made.astype(BF16)


def run_expert(x, order, pieces_a, pieces_b):
    rows, width = x.shape
    ff = order.shape[0]
    shards = 4 * pieces_a[0].shape[0]
    return pl.pallas_call(
        expert_kernel,
        out_shape=jax.ShapeDtypeStruct((rows, width), BF16),
        in_specs=[VMEM, VMEM] + [ANY] * 8,
        out_specs=VMEM,
        scratch_shapes=[
            pltpu.VMEM((shards, 16, 2 * width), BF16),
            pltpu.VMEM((shards, 8, 2 * width), BF16),
            pltpu.VMEM((shards, width // shards, ff), BF16),
            pltpu.VMEM((rows, ff), BF16),
            pltpu.SemaphoreType.DMA((4,)),
            pltpu.SemaphoreType.DMA((32,)),
            pltpu.SemaphoreType.DMA((32,)),
        ],
        compiler_params=pltpu.CompilerParams(vmem_limit_bytes=55 << 20),
        cost_estimate=pl.CostEstimate(
            flops=6 * rows * width * ff,
            bytes_accessed=6 * width * ff + 4 * x.size,
            transcendentals=rows * ff,
        ),
        name="expert",
    )(x, order, *pieces_a, *pieces_b)


def last_kernel(expert_ref, probs_ref, x_ref, out_ref, *, ring, cap):
    expert = expert_ref[...]
    count = expert.shape[0]
    member = lax.broadcasted_iota(jnp.int32, (count, ring), 1) == expert
    before = lax.broadcasted_iota(jnp.int32, (count, count), 1) < lax.broadcasted_iota(
        jnp.int32, (count, count), 0
    )
    earlier = lax.dot_general(
        before.astype(F32), member.astype(F32), NN, preferred_element_type=F32
    )
    slot = jnp.sum(jnp.where(member, earlier, 0.0), axis=1, keepdims=True).astype(jnp.int32)
    place = expert * cap + slot
    pick = lax.broadcasted_iota(jnp.int32, (count, ring * cap), 1) == place
    probs = probs_ref[...]
    share = probs[:, :1] / jnp.sum(probs, axis=1, keepdims=True)
    got = lax.dot_general(
        pick.astype(F32).astype(BF16), x_ref[...], NN, preferred_element_type=F32
    )
    out_ref[...] = (share * got).astype(BF16)


def exchange(x, ring):
    blocks = x.reshape(ring, x.shape[0] // ring, x.shape[1])
    return lax.all_to_all(blocks, "expert", split_axis=0, concat_axis=0, tiled=True).reshape(x.shape)


def local(tokens, norm_gain, route_probs, window_expert, w_gate_up, w_down):
    tok_count, width = tokens.shape
    ring = lax.axis_size("expert")
    cap = 3 * tok_count // ring
    rows = ring * cap
    ff = w_down.shape[2]
    sent = pl.pallas_call(
        functools.partial(send_kernel, ring=ring, cap=cap),
        out_shape=jax.ShapeDtypeStruct((rows, width), BF16),
        in_specs=[VMEM] * 3,
        out_specs=VMEM,
        compiler_params=pltpu.CompilerParams(vmem_limit_bytes=20 << 20),
        cost_estimate=pl.CostEstimate(
            flops=6 * tok_count * tok_count * width,
            bytes_accessed=8 * tokens.size,
            transcendentals=0,
        ),
        name="send",
    )(tokens, norm_gain[None, :], window_expert[None, :])
    x = exchange(sent, ring)
    mine_a, mine_b = pl.pallas_call(
        pack_kernel,
        out_shape=[
            jax.ShapeDtypeStruct((1, 16, 2 * width), BF16),
            jax.ShapeDtypeStruct((1, 64, 1280), BF16),
        ],
        in_specs=[VMEM] * 2,
        out_specs=[VMEM] * 2,
        name="pack",
    )(w_gate_up[0], w_down[0])
    made = run_expert(x, hidden_order(ff), *gather(mine_a, mine_b))
    return pl.pallas_call(
        functools.partial(last_kernel, ring=ring, cap=cap),
        out_shape=jax.ShapeDtypeStruct((tok_count, width), BF16),
        in_specs=[VMEM] * 3,
        out_specs=VMEM,
        cost_estimate=pl.CostEstimate(
            flops=6 * tok_count * tok_count * width, bytes_accessed=8 * tokens.size, transcendentals=0
        ),
        compiler_params=pltpu.CompilerParams(vmem_limit_bytes=16 << 20),
        name="last",
    )(window_expert[:, None], route_probs, exchange(made, ring))


def solution(mesh):
    placed = (
        P(("dp", "expert"), None),
        P(),
        P(("dp", "expert"), None),
        P(("dp", "expert")),
        P("expert", "dp", None),
        P("expert", "dp", None),
    )
    return jax.shard_map(
        local, mesh=mesh, in_specs=placed, out_specs=P(("dp", "expert"), None), check_vma=False
    )
```

```python
import functools

import jax
import jax.numpy as jnp
import numpy as np
from jax import lax
from jax.experimental import pallas as pl
from jax.experimental.pallas import tpu as pltpu
from jax.sharding import PartitionSpec as P

F32, BF16 = jnp.float32, jnp.bfloat16
NT = (((1,), (1,)), ((), ()))
NN = (((1,), (0,)), ((), ()))
VMEM = pl.BlockSpec(memory_space=pltpu.VMEM)
HBM = pl.BlockSpec(memory_space=pltpu.HBM)
ANY = pl.BlockSpec(memory_space=pl.ANY)


def trade(x, where):
    return lax.ppermute(x, "dp", [(i, where(i)) for i in range(lax.axis_size("dp"))])


def flip(mask):
    return lambda i: i ^ mask


def turn(bit, hops):
    return lambda i: (i & ~(3 << bit)) | ((((i >> bit) + hops) & 3) << bit)


X_BIT, Y_BIT, CORE = 3, 1, 1
GRAY = (0, 1, 3, 2)
TURNS = (0, -1, 1, 2)


def gather(a, b):
    for step in (1, 3):
        a_in, b_in = lax.optimization_barrier(
            (trade(a, flip(step << X_BIT)), trade(b, flip(step << Y_BIT)))
        )
        a, b = jnp.concatenate([a, a_in], axis=0), jnp.concatenate([b, b_in], axis=0)
    a_l, b_l, a_r, b_r = lax.optimization_barrier(
        (
            trade(a, turn(Y_BIT, 1)),
            trade(b, turn(X_BIT, 1)),
            trade(a, turn(Y_BIT, -1)),
            trade(b, turn(X_BIT, -1)),
        )
    )
    a12, b12 = jnp.concatenate([a, a_l, a_r], axis=0), jnp.concatenate([b, b_l, b_r], axis=0)
    a_0, b_0, a_1, b_1 = (
        trade(a_l[:2], turn(Y_BIT, 1)),
        trade(b_l[:2], turn(X_BIT, 1)),
        trade(a_r[2:], turn(Y_BIT, -1)),
        trade(b_r[2:], turn(X_BIT, -1)),
    )
    a4, b4 = jnp.concatenate([a_0, a_1], axis=0), jnp.concatenate([b_0, b_1], axis=0)
    near = flip(CORE)
    return (a12, a4, trade(a12, near), trade(a4, near)), (b12, b4, trade(b12, near), trade(b4, near))


def shard_of(me, slot, x_first):
    x, y, core = me >> X_BIT, (me >> Y_BIT) & 3, me & 1
    group, k = (slot >> 2) & 3, slot & 3
    if x_first:
        x, y = x ^ GRAY[k], (y + TURNS[group]) & 3
    else:
        x, y = (x + TURNS[group]) & 3, y ^ GRAY[k]
    return (x << X_BIT) | (y << Y_BIT) | (core ^ (slot >> 4))


def hidden_order(ff):
    me = lax.axis_index("dp")
    k = np.arange(ff)
    x_first = k < 512
    slot = np.where(x_first, k >> 4, (k - 512) >> 3)
    low = np.where(x_first, k & 15, 16 + (k & 7))
    pair, ring = np.array(GRAY)[slot & 3], np.array(TURNS)[(slot >> 2) & 3]
    x = (((me >> X_BIT) ^ np.where(x_first, pair, 0)) + np.where(x_first, 0, ring)) & 3
    y = ((((me >> Y_BIT) & 3) ^ np.where(x_first, 0, pair)) + np.where(x_first, ring, 0)) & 3
    shard = (x << X_BIT) | (y << Y_BIT) | ((me & 1) ^ (slot >> 4))
    unit = (shard * 24 + low).astype(jnp.int32)
    return (unit[:, None] == jnp.arange(ff, dtype=jnp.int32)[None, :]).astype(BF16)


def pack_kernel(both_ref, down_ref, a_ref, b_ref):
    a_ref[0] = both_ref[:16]
    b_ref[0, :, :768] = down_ref[...]
    for j in range(8):
        b_ref[0, 8 * j : 8 * (j + 1), 768:] = both_ref[16:, 512 * j : 512 * (j + 1)]


def send_kernel(tok_hbm, gain_hbm, expert_hbm, out_ref, tok_ref, gain_ref, expert_ref, sems, *, ring, cap):
    copies = [
        pltpu.make_async_copy(source, target, sems.at[i])
        for i, (source, target) in enumerate(
            ((tok_hbm, tok_ref), (gain_hbm, gain_ref), (expert_hbm, expert_ref))
        )
    ]
    for copy in copies:
        copy.start()
    for copy in copies:
        copy.wait()
    values = tok_ref[...].astype(F32)
    meansq = jnp.mean(values * values, axis=1, keepdims=True)
    normed = (values * lax.rsqrt(meansq + 1e-06) * gain_ref[...]).astype(BF16)
    expert = expert_ref[...]
    count = expert.shape[1]
    member = lax.broadcasted_iota(jnp.int32, (ring, count), 0) == expert
    before = lax.broadcasted_iota(jnp.int32, (count, count), 0) < lax.broadcasted_iota(
        jnp.int32, (count, count), 1
    )
    earlier = lax.dot_general(
        member.astype(F32), before.astype(F32), NN, preferred_element_type=F32
    )
    slot = jnp.sum(jnp.where(member, earlier, 0.0), axis=0, keepdims=True).astype(jnp.int32)
    place = expert * cap + slot
    pick = lax.broadcasted_iota(jnp.int32, (ring * cap, count), 0) == place
    out_ref[...] = lax.dot_general(
        pick.astype(F32).astype(BF16), normed, NN, preferred_element_type=F32
    ).astype(BF16)


def expert_kernel(x_hbm, order_ref, *rest):
    pieces_a, pieces_b = rest[:4], rest[4:8]
    out_hbm, x_ref, out_ref, wa, wb, wd, hid, sem_x, sem_a, sem_b, sem_d, sem_o = rest[8:]
    width = x_ref.shape[1]
    me = lax.axis_index("dp")
    copy_x = pltpu.make_async_copy(x_hbm, x_ref, sem_x)
    copies_a, copies_b, copies_d = [], [], []
    start = 0
    for q, (piece_a, piece_b) in enumerate(zip(pieces_a, pieces_b)):
        each = piece_a.shape[0]
        copies_a.append(
            pltpu.make_async_copy(piece_a, wa.at[pl.ds(start, each)], sem_a.at[q])
        )
        for j in range(8):
            copies_b.append(
                pltpu.make_async_copy(
                    piece_b.at[:, pl.ds(8 * j, 8), pl.ds(768, 512)],
                    wb.at[pl.ds(start, each), :, pl.ds(512 * j, 512)],
                    sem_b.at[8 * q + j],
                )
            )
        for p in range(each):
            slot = start + p
            copies_d.append(
                pltpu.make_async_copy(
                    piece_b.at[p, :, pl.ds(0, 768)],
                    wd.at[shard_of(me, slot, False)],
                    sem_d.at[slot],
                )
            )
        start += each
    for copy in [copy_x] + copies_a + copies_b + copies_d:
        copy.start()
    copy_x.wait()
    x = x_ref[...]

    def units(w, cols):
        gate = lax.dot_general(x, w[:, :width], NT, preferred_element_type=F32)
        upper = lax.dot_general(x, w[:, width:], NT, preferred_element_type=F32)
        hid[:, cols] = (gate / (1.0 + jnp.exp(-gate)) * upper).astype(BF16)

    for c in range(2):
        copies_a[2 * c].wait()
        copies_a[2 * c + 1].wait()
        units(wa[16 * c : 16 * (c + 1)].reshape(256, 2 * width), slice(256 * c, 256 * (c + 1)))
    for copy in copies_b:
        copy.wait()
    units(wb[...].reshape(256, 2 * width), slice(512, 768))
    hidden = lax.dot_general(hid[...], order_ref[...], NN, preferred_element_type=F32).astype(BF16)
    for copy in copies_d:
        copy.wait()
    shards, feats, ff = wd.shape
    group = shards // sem_o.shape[0]
    copies_o = []
    for n in range(shards // group):
        down = wd[group * n : group * (n + 1)].reshape(group * feats, ff)
        cols = pl.ds(group * feats * n, group * feats)
        out_ref[:, cols] = lax.dot_general(
            hidden, down, NT, preferred_element_type=F32
        ).astype(BF16)
        copies_o.append(
            pltpu.make_async_copy(out_ref.at[:, cols], out_hbm.at[:, cols], sem_o.at[n])
        )
        copies_o[-1].start()
    for copy in copies_o:
        copy.wait()


def run_expert(x, order, pieces_a, pieces_b):
    rows, width = x.shape
    ff = order.shape[0]
    shards = 32
    return pl.pallas_call(
        expert_kernel,
        out_shape=jax.ShapeDtypeStruct((rows, width), BF16),
        in_specs=[ANY, VMEM] + [ANY] * 8,
        out_specs=ANY,
        scratch_shapes=[
            pltpu.VMEM((rows, width), BF16),
            pltpu.VMEM((rows, width), BF16),
            pltpu.VMEM((shards, 16, 2 * width), BF16),
            pltpu.VMEM((shards, 8, 2 * width), BF16),
            pltpu.VMEM((shards, width // shards, ff), BF16),
            pltpu.VMEM((rows, ff), BF16),
            pltpu.SemaphoreType.DMA,
            pltpu.SemaphoreType.DMA((4,)),
            pltpu.SemaphoreType.DMA((32,)),
            pltpu.SemaphoreType.DMA((32,)),
            pltpu.SemaphoreType.DMA((4,)),
        ],
        compiler_params=pltpu.CompilerParams(vmem_limit_bytes=46 << 20),
        cost_estimate=pl.CostEstimate(
            flops=6 * rows * width * ff,
            bytes_accessed=6 * width * ff + 4 * x.size,
            transcendentals=rows * ff,
        ),
        name="expert",
    )(x, order, *pieces_a, *pieces_b)


def last_kernel(expert_ref, probs_ref, x_ref, out_ref, *, ring, cap):
    expert = expert_ref[...]
    count = expert.shape[0]
    member = lax.broadcasted_iota(jnp.int32, (count, ring), 1) == expert
    before = lax.broadcasted_iota(jnp.int32, (count, count), 1) < lax.broadcasted_iota(
        jnp.int32, (count, count), 0
    )
    earlier = lax.dot_general(
        before.astype(F32), member.astype(F32), NN, preferred_element_type=F32
    )
    slot = jnp.sum(jnp.where(member, earlier, 0.0), axis=1, keepdims=True).astype(jnp.int32)
    place = expert * cap + slot
    pick = lax.broadcasted_iota(jnp.int32, (count, ring * cap), 1) == place
    probs = probs_ref[...]
    share = probs[:, :1] / jnp.sum(probs, axis=1, keepdims=True)
    got = lax.dot_general(
        pick.astype(F32).astype(BF16), x_ref[...], NN, preferred_element_type=F32
    )
    out_ref[...] = (share * got).astype(BF16)


def exchange(x, ring):
    blocks = x.reshape(ring, x.shape[0] // ring, x.shape[1])
    return lax.all_to_all(blocks, "expert", split_axis=0, concat_axis=0, tiled=True).reshape(x.shape)


def local(tokens, norm_gain, route_probs, window_expert, w_gate_up, w_down):
    tok_count, width = tokens.shape
    ring = lax.axis_size("expert")
    cap = 3 * tok_count // ring
    rows = ring * cap
    ff = w_down.shape[2]
    sent = pl.pallas_call(
        functools.partial(send_kernel, ring=ring, cap=cap),
        out_shape=jax.ShapeDtypeStruct((rows, width), BF16),
        in_specs=[ANY] * 3,
        out_specs=VMEM,
        scratch_shapes=[
            pltpu.VMEM((tok_count, width), BF16),
            pltpu.VMEM((1, width), F32),
            pltpu.VMEM((1, tok_count), jnp.int32),
            pltpu.SemaphoreType.DMA((3,)),
        ],
        compiler_params=pltpu.CompilerParams(vmem_limit_bytes=20 << 20),
        cost_estimate=pl.CostEstimate(
            flops=6 * tok_count * tok_count * width,
            bytes_accessed=8 * tokens.size,
            transcendentals=0,
        ),
        name="send",
    )(tokens, norm_gain[None, :], window_expert[None, :])
    w_gate_up, w_down, sent = lax.optimization_barrier((w_gate_up, w_down, sent))
    x = exchange(sent, ring)
    mine_a, mine_b = pl.pallas_call(
        pack_kernel,
        out_shape=[
            jax.ShapeDtypeStruct((1, 16, 2 * width), BF16),
            jax.ShapeDtypeStruct((1, 64, 1280), BF16),
        ],
        in_specs=[VMEM] * 2,
        out_specs=[VMEM] * 2,
        name="pack",
    )(w_gate_up[0], w_down[0])
    made = run_expert(x, hidden_order(ff), *gather(mine_a, mine_b))
    return pl.pallas_call(
        functools.partial(last_kernel, ring=ring, cap=cap),
        out_shape=jax.ShapeDtypeStruct((tok_count, width), BF16),
        in_specs=[VMEM] * 3,
        out_specs=VMEM,
        cost_estimate=pl.CostEstimate(
            flops=6 * tok_count * tok_count * width, bytes_accessed=8 * tokens.size, transcendentals=0
        ),
        compiler_params=pltpu.CompilerParams(vmem_limit_bytes=16 << 20),
        name="last",
    )(window_expert[:, None], route_probs, exchange(made, ring))


def solution(mesh):
    placed = (
        P(("dp", "expert"), None),
        P(),
        P(("dp", "expert"), None),
        P(("dp", "expert")),
        P("expert", "dp", None),
        P("expert", "dp", None),
    )
    return jax.shard_map(
        local, mesh=mesh, in_specs=placed, out_specs=P(("dp", "expert"), None), check_vma=False
    )
```

```python
import functools

import jax
import jax.numpy as jnp
import numpy as np
from jax import lax
from jax.experimental import pallas as pl
from jax.experimental.pallas import tpu as pltpu
from jax.sharding import PartitionSpec as P

F32, BF16 = jnp.float32, jnp.bfloat16
NT = (((1,), (1,)), ((), ()))
NN = (((1,), (0,)), ((), ()))
VMEM = pl.BlockSpec(memory_space=pltpu.VMEM)
HBM = pl.BlockSpec(memory_space=pltpu.HBM)
ANY = pl.BlockSpec(memory_space=pl.ANY)


def trade(x, where):
    return lax.ppermute(x, "dp", [(i, where(i)) for i in range(lax.axis_size("dp"))])


def flip(mask):
    return lambda i: i ^ mask


def turn(bit, hops):
    return lambda i: (i & ~(3 << bit)) | ((((i >> bit) + hops) & 3) << bit)


X_BIT, Y_BIT, CORE = 3, 1, 1
GRAY = (0, 1, 3, 2)
TURNS = (0, -1, 1, 2)


def gather(a, b):
    for step in (1, 3):
        a_in, b_in = lax.optimization_barrier(
            (trade(a, flip(step << X_BIT)), trade(b, flip(step << Y_BIT)))
        )
        a, b = jnp.concatenate([a, a_in], axis=0), jnp.concatenate([b, b_in], axis=0)
    a_l, b_l, a_r, b_r = lax.optimization_barrier(
        (
            trade(a, turn(Y_BIT, 1)),
            trade(b, turn(X_BIT, 1)),
            trade(a, turn(Y_BIT, -1)),
            trade(b, turn(X_BIT, -1)),
        )
    )
    a12, b12 = jnp.concatenate([a, a_l, a_r], axis=0), jnp.concatenate([b, b_l, b_r], axis=0)
    a_0, b_0, a_1, b_1 = (
        trade(a_l[:2], turn(Y_BIT, 1)),
        trade(b_l[:2], turn(X_BIT, 1)),
        trade(a_r[2:], turn(Y_BIT, -1)),
        trade(b_r[2:], turn(X_BIT, -1)),
    )
    a4, b4 = jnp.concatenate([a_0, a_1], axis=0), jnp.concatenate([b_0, b_1], axis=0)
    near = flip(CORE)
    return (a12, a4, trade(a12, near), trade(a4, near)), (b12, b4, trade(b12, near), trade(b4, near))


def shard_of(me, slot, x_first):
    x, y, core = me >> X_BIT, (me >> Y_BIT) & 3, me & 1
    group, k = (slot >> 2) & 3, slot & 3
    if x_first:
        x, y = x ^ GRAY[k], (y + TURNS[group]) & 3
    else:
        x, y = (x + TURNS[group]) & 3, y ^ GRAY[k]
    return (x << X_BIT) | (y << Y_BIT) | (core ^ (slot >> 4))


def hidden_order(ff):
    me = lax.axis_index("dp")
    k = np.arange(ff)
    x_first = k < 512
    slot = np.where(x_first, k >> 4, (k - 512) >> 3)
    low = np.where(x_first, k & 15, 16 + (k & 7))
    pair, ring = np.array(GRAY)[slot & 3], np.array(TURNS)[(slot >> 2) & 3]
    x = (((me >> X_BIT) ^ np.where(x_first, pair, 0)) + np.where(x_first, 0, ring)) & 3
    y = ((((me >> Y_BIT) & 3) ^ np.where(x_first, 0, pair)) + np.where(x_first, ring, 0)) & 3
    shard = (x << X_BIT) | (y << Y_BIT) | ((me & 1) ^ (slot >> 4))
    unit = (shard * 24 + low).astype(jnp.int32)
    return (unit[:, None] == jnp.arange(ff, dtype=jnp.int32)[None, :]).astype(BF16)


def prepare_kernel(*refs, ring, cap):
    tok_hbm, gain_hbm, expert_hbm, both_hbm, down_hbm = refs[:5]
    out_ref, a_ref, b_ref, tok_ref, gain_ref, expert_ref, sems = refs[5:]
    moves = [
        (tok_hbm, tok_ref),
        (gain_hbm, gain_ref),
        (expert_hbm, expert_ref),
        (both_hbm.at[pl.ds(0, 16)], a_ref.at[0]),
        (down_hbm, b_ref.at[0, :, pl.ds(0, 768)]),
    ] + [
        (both_hbm.at[pl.ds(16, 8), pl.ds(512 * j, 512)], b_ref.at[0, pl.ds(8 * j, 8), pl.ds(768, 512)])
        for j in range(8)
    ]
    copies = [pltpu.make_async_copy(*move, sems.at[i]) for i, move in enumerate(moves)]
    for copy in copies:
        copy.start()
    for copy in copies[:3]:
        copy.wait()
    values = tok_ref[...].astype(F32)
    meansq = jnp.mean(values * values, axis=1, keepdims=True)
    normed = (values * lax.rsqrt(meansq + 1e-06) * gain_ref[...]).astype(BF16)
    expert = expert_ref[...]
    count = expert.shape[1]
    member = lax.broadcasted_iota(jnp.int32, (ring, count), 0) == expert
    before = lax.broadcasted_iota(jnp.int32, (count, count), 0) < lax.broadcasted_iota(
        jnp.int32, (count, count), 1
    )
    earlier = lax.dot_general(
        member.astype(F32), before.astype(F32), NN, preferred_element_type=F32
    )
    slot = jnp.sum(jnp.where(member, earlier, 0.0), axis=0, keepdims=True).astype(jnp.int32)
    place = expert * cap + slot
    pick = lax.broadcasted_iota(jnp.int32, (ring * cap, count), 0) == place
    out_ref[...] = lax.dot_general(
        pick.astype(F32).astype(BF16), normed, NN, preferred_element_type=F32
    ).astype(BF16)
    for copy in copies[3:]:
        copy.wait()


def expert_kernel(x_hbm, order_ref, *rest):
    pieces_a, pieces_b = rest[:4], rest[4:8]
    out_hbm, x_ref, out_ref, wa, wb, wd, hid, sem_x, sem_a, sem_b, sem_d, sem_o = rest[8:]
    width = x_ref.shape[1]
    me = lax.axis_index("dp")
    copy_x = pltpu.make_async_copy(x_hbm, x_ref, sem_x)
    copies_a, copies_b, copies_d = [], [], []
    start = 0
    for q, (piece_a, piece_b) in enumerate(zip(pieces_a, pieces_b)):
        each = piece_a.shape[0]
        copies_a.append(
            pltpu.make_async_copy(piece_a, wa.at[pl.ds(start, each)], sem_a.at[q])
        )
        for j in range(8):
            copies_b.append(
                pltpu.make_async_copy(
                    piece_b.at[:, pl.ds(8 * j, 8), pl.ds(768, 512)],
                    wb.at[pl.ds(start, each), :, pl.ds(512 * j, 512)],
                    sem_b.at[8 * q + j],
                )
            )
        for p in range(each):
            slot = start + p
            copies_d.append(
                pltpu.make_async_copy(
                    piece_b.at[p, :, pl.ds(0, 768)],
                    wd.at[shard_of(me, slot, False)],
                    sem_d.at[slot],
                )
            )
        start += each
    for copy in [copy_x] + copies_a + copies_b + copies_d:
        copy.start()
    copy_x.wait()
    x = x_ref[...]

    def units(w, cols):
        gate = lax.dot_general(x, w[:, :width], NT, preferred_element_type=F32)
        upper = lax.dot_general(x, w[:, width:], NT, preferred_element_type=F32)
        hid[:, cols] = (gate / (1.0 + jnp.exp(-gate)) * upper).astype(BF16)

    for c in range(2):
        copies_a[2 * c].wait()
        copies_a[2 * c + 1].wait()
        units(wa[16 * c : 16 * (c + 1)].reshape(256, 2 * width), slice(256 * c, 256 * (c + 1)))
    for copy in copies_b:
        copy.wait()
    units(wb[...].reshape(256, 2 * width), slice(512, 768))
    hidden = lax.dot_general(hid[...], order_ref[...], NN, preferred_element_type=F32).astype(BF16)
    for copy in copies_d:
        copy.wait()
    shards, feats, ff = wd.shape
    group = shards // sem_o.shape[0]
    copies_o = []
    for n in range(shards // group):
        down = wd[group * n : group * (n + 1)].reshape(group * feats, ff)
        cols = pl.ds(group * feats * n, group * feats)
        out_ref[:, cols] = lax.dot_general(
            hidden, down, NT, preferred_element_type=F32
        ).astype(BF16)
        copies_o.append(
            pltpu.make_async_copy(out_ref.at[:, cols], out_hbm.at[:, cols], sem_o.at[n])
        )
        copies_o[-1].start()
    for copy in copies_o:
        copy.wait()


def run_expert(x, order, pieces_a, pieces_b):
    rows, width = x.shape
    ff = order.shape[0]
    shards = 32
    return pl.pallas_call(
        expert_kernel,
        out_shape=jax.ShapeDtypeStruct((rows, width), BF16),
        in_specs=[ANY, VMEM] + [ANY] * 8,
        out_specs=ANY,
        scratch_shapes=[
            pltpu.VMEM((rows, width), BF16),
            pltpu.VMEM((rows, width), BF16),
            pltpu.VMEM((shards, 16, 2 * width), BF16),
            pltpu.VMEM((shards, 8, 2 * width), BF16),
            pltpu.VMEM((shards, width // shards, ff), BF16),
            pltpu.VMEM((rows, ff), BF16),
            pltpu.SemaphoreType.DMA,
            pltpu.SemaphoreType.DMA((4,)),
            pltpu.SemaphoreType.DMA((32,)),
            pltpu.SemaphoreType.DMA((32,)),
            pltpu.SemaphoreType.DMA((4,)),
        ],
        compiler_params=pltpu.CompilerParams(vmem_limit_bytes=46 << 20),
        cost_estimate=pl.CostEstimate(
            flops=6 * rows * width * ff,
            bytes_accessed=6 * width * ff + 4 * x.size,
            transcendentals=rows * ff,
        ),
        name="expert",
    )(x, order, *pieces_a, *pieces_b)


def last_kernel(expert_ref, probs_ref, x_ref, out_ref, *, ring, cap):
    expert = expert_ref[...]
    count = expert.shape[0]
    member = lax.broadcasted_iota(jnp.int32, (count, ring), 1) == expert
    before = lax.broadcasted_iota(jnp.int32, (count, count), 1) < lax.broadcasted_iota(
        jnp.int32, (count, count), 0
    )
    earlier = lax.dot_general(
        before.astype(F32), member.astype(F32), NN, preferred_element_type=F32
    )
    slot = jnp.sum(jnp.where(member, earlier, 0.0), axis=1, keepdims=True).astype(jnp.int32)
    place = expert * cap + slot
    pick = lax.broadcasted_iota(jnp.int32, (count, ring * cap), 1) == place
    probs = probs_ref[...]
    share = probs[:, :1] / jnp.sum(probs, axis=1, keepdims=True)
    got = lax.dot_general(
        pick.astype(F32).astype(BF16), x_ref[...], NN, preferred_element_type=F32
    )
    out_ref[...] = (share * got).astype(BF16)


def exchange(x, ring):
    blocks = x.reshape(ring, x.shape[0] // ring, x.shape[1])
    return lax.all_to_all(blocks, "expert", split_axis=0, concat_axis=0, tiled=True).reshape(x.shape)


def local(tokens, norm_gain, route_probs, window_expert, w_gate_up, w_down):
    tok_count, width = tokens.shape
    ring = lax.axis_size("expert")
    cap = 3 * tok_count // ring
    rows = ring * cap
    ff = w_down.shape[2]
    sent, mine_a, mine_b = pl.pallas_call(
        functools.partial(prepare_kernel, ring=ring, cap=cap),
        out_shape=[
            jax.ShapeDtypeStruct((rows, width), BF16),
            jax.ShapeDtypeStruct((1, 16, 2 * width), BF16),
            jax.ShapeDtypeStruct((1, 64, 1280), BF16),
        ],
        in_specs=[ANY] * 5,
        out_specs=[VMEM] * 3,
        scratch_shapes=[
            pltpu.VMEM((tok_count, width), BF16),
            pltpu.VMEM((1, width), F32),
            pltpu.VMEM((1, tok_count), jnp.int32),
            pltpu.SemaphoreType.DMA((13,)),
        ],
        compiler_params=pltpu.CompilerParams(vmem_limit_bytes=60 << 20),
        cost_estimate=pl.CostEstimate(
            flops=6 * tok_count * tok_count * width,
            bytes_accessed=8 * tokens.size,
            transcendentals=0,
        ),
        name="prepare",
    )(tokens, norm_gain[None, :], window_expert[None, :], w_gate_up[0], w_down[0])
    x = exchange(sent, ring)
    made = run_expert(x, hidden_order(ff), *gather(mine_a, mine_b))
    return pl.pallas_call(
        functools.partial(last_kernel, ring=ring, cap=cap),
        out_shape=jax.ShapeDtypeStruct((tok_count, width), BF16),
        in_specs=[VMEM] * 3,
        out_specs=VMEM,
        cost_estimate=pl.CostEstimate(
            flops=6 * tok_count * tok_count * width, bytes_accessed=8 * tokens.size, transcendentals=0
        ),
        compiler_params=pltpu.CompilerParams(vmem_limit_bytes=16 << 20),
        name="last",
    )(window_expert[:, None], route_probs, exchange(made, ring))


def solution(mesh):
    placed = (
        P(("dp", "expert"), None),
        P(),
        P(("dp", "expert"), None),
        P(("dp", "expert")),
        P("expert", "dp", None),
        P("expert", "dp", None),
    )
    return jax.shard_map(
        local, mesh=mesh, in_specs=placed, out_specs=P(("dp", "expert"), None), check_vma=False
    )
```

```python
import functools

import jax
import jax.numpy as jnp
import numpy as np
from jax import lax
from jax.experimental import pallas as pl
from jax.experimental.pallas import tpu as pltpu
from jax.sharding import PartitionSpec as P

F32, BF16 = jnp.float32, jnp.bfloat16
NT = (((1,), (1,)), ((), ()))
NN = (((1,), (0,)), ((), ()))
VMEM = pl.BlockSpec(memory_space=pltpu.VMEM)
HBM = pl.BlockSpec(memory_space=pltpu.HBM)
ANY = pl.BlockSpec(memory_space=pl.ANY)


def trade(x, where):
    return lax.ppermute(x, "dp", [(i, where(i)) for i in range(lax.axis_size("dp"))])


def flip(mask):
    return lambda i: i ^ mask


def turn(bit, hops):
    return lambda i: (i & ~(3 << bit)) | ((((i >> bit) + hops) & 3) << bit)


X_BIT, Y_BIT, CORE = 3, 1, 1
GRAY = (0, 1, 3, 2)
TURNS = (0, -1, 1, 2)


def gather(a, b):
    for step in (1, 3):
        a_in = trade(a, flip(step << X_BIT))
        if step == 1:
            a_in, b = lax.optimization_barrier((a_in, b))
        a_in, b_in = lax.optimization_barrier((a_in, trade(b, flip(step << Y_BIT))))
        a, b = jnp.concatenate([a, a_in], axis=0), jnp.concatenate([b, b_in], axis=0)
    near = flip(CORE)
    a_l, b_l, a_r, b_r, a_near, b_near = lax.optimization_barrier(
        (
            trade(a, turn(Y_BIT, 1)),
            trade(b, turn(X_BIT, 1)),
            trade(a, turn(Y_BIT, -1)),
            trade(b, turn(X_BIT, -1)),
            trade(a, near),
            trade(b, near),
        )
    )
    a8, b8 = jnp.concatenate([a_l, a_r], axis=0), jnp.concatenate([b_l, b_r], axis=0)
    a_0, b_0, a_1, b_1 = (
        trade(a_l[:2], turn(Y_BIT, 1)),
        trade(b_l[:2], turn(X_BIT, 1)),
        trade(a_r[2:], turn(Y_BIT, -1)),
        trade(b_r[2:], turn(X_BIT, -1)),
    )
    a4, b4 = jnp.concatenate([a_0, a_1], axis=0), jnp.concatenate([b_0, b_1], axis=0)
    return (
        (a, a8, a4, a_near, trade(a8, near), trade(a4, near)),
        (b, b8, b4, b_near, trade(b8, near), trade(b4, near)),
    )


def shard_of(me, slot, x_first):
    x, y, core = me >> X_BIT, (me >> Y_BIT) & 3, me & 1
    group, k = (slot >> 2) & 3, slot & 3
    if x_first:
        x, y = x ^ GRAY[k], (y + TURNS[group]) & 3
    else:
        x, y = (x + TURNS[group]) & 3, y ^ GRAY[k]
    return (x << X_BIT) | (y << Y_BIT) | (core ^ (slot >> 4))


def hidden_order(ff):
    me = lax.axis_index("dp")
    k = np.arange(ff)
    x_first = k < 512
    slot = np.where(x_first, k >> 4, (k - 512) >> 3)
    low = np.where(x_first, k & 15, 16 + (k & 7))
    pair, ring = np.array(GRAY)[slot & 3], np.array(TURNS)[(slot >> 2) & 3]
    x = (((me >> X_BIT) ^ np.where(x_first, pair, 0)) + np.where(x_first, 0, ring)) & 3
    y = ((((me >> Y_BIT) & 3) ^ np.where(x_first, 0, pair)) + np.where(x_first, ring, 0)) & 3
    shard = (x << X_BIT) | (y << Y_BIT) | ((me & 1) ^ (slot >> 4))
    unit = (shard * 24 + low).astype(jnp.int32)
    return (unit[:, None] == jnp.arange(ff, dtype=jnp.int32)[None, :]).astype(BF16)


def prepare_kernel(*refs, ring, cap):
    tok_hbm, gain_hbm, expert_hbm, both_hbm, down_hbm = refs[:5]
    out_hbm, a_ref, b_ref, out_ref, tok_ref, gain_ref, expert_ref, sems, sem_o = refs[5:]
    moves = [
        (tok_hbm, tok_ref),
        (gain_hbm, gain_ref),
        (expert_hbm, expert_ref),
        (both_hbm.at[pl.ds(0, 16)], a_ref.at[0]),
        (down_hbm, b_ref.at[0, :, pl.ds(0, 768)]),
    ] + [
        (both_hbm.at[pl.ds(16, 8), pl.ds(512 * j, 512)], b_ref.at[0, pl.ds(8 * j, 8), pl.ds(768, 512)])
        for j in range(8)
    ]
    copies = [pltpu.make_async_copy(*move, sems.at[i]) for i, move in enumerate(moves)]
    for copy in copies:
        copy.start()
    for copy in copies[:3]:
        copy.wait()
    values = tok_ref[...].astype(F32)
    meansq = jnp.mean(values * values, axis=1, keepdims=True)
    normed = (values * lax.rsqrt(meansq + 1e-06) * gain_ref[...]).astype(BF16)
    expert = expert_ref[...]
    count = expert.shape[1]
    member = lax.broadcasted_iota(jnp.int32, (ring, count), 0) == expert
    before = lax.broadcasted_iota(jnp.int32, (count, count), 0) < lax.broadcasted_iota(
        jnp.int32, (count, count), 1
    )
    earlier = lax.dot_general(
        member.astype(F32), before.astype(F32), NN, preferred_element_type=F32
    )
    slot = jnp.sum(jnp.where(member, earlier, 0.0), axis=0, keepdims=True).astype(jnp.int32)
    place = expert * cap + slot
    parts = sem_o.shape[0]
    part = ring * cap // parts
    for n in range(parts):
        rows = pl.ds(n * part, part)
        pick = lax.broadcasted_iota(jnp.int32, (part, count), 0) + n * part == place
        out_ref[rows] = lax.dot_general(
            pick.astype(F32).astype(BF16), normed, NN, preferred_element_type=F32
        ).astype(BF16)
        copies.append(pltpu.make_async_copy(out_ref.at[rows], out_hbm.at[rows], sem_o.at[n]))
        copies[-1].start()
    for copy in copies[3:]:
        copy.wait()


def expert_kernel(x_ref, order_ref, *rest):
    pieces_a, pieces_b = rest[:6], rest[6:12]
    out_hbm, out_ref, wa, wb, wd, hid, sem_a, sem_b, sem_d, sem_o = rest[12:]
    width = x_ref.shape[1]
    me = lax.axis_index("dp")
    copies_a, copies_b, copies_d = [], [], []
    start = 0
    for q, (piece_a, piece_b) in enumerate(zip(pieces_a, pieces_b)):
        each = piece_a.shape[0]
        for p in range(0, each, 4):
            copies_a.append(
                pltpu.make_async_copy(
                    piece_a.at[pl.ds(p, 4)], wa.at[pl.ds(start + p, 4)], sem_a.at[(start + p) // 4]
                )
            )
        for j in range(8):
            copies_b.append(
                pltpu.make_async_copy(
                    piece_b.at[:, pl.ds(8 * j, 8), pl.ds(768, 512)],
                    wb.at[pl.ds(start, each), :, pl.ds(512 * j, 512)],
                    sem_b.at[8 * q + j],
                )
            )
        for p in range(each):
            slot = start + p
            copies_d.append(
                pltpu.make_async_copy(
                    piece_b.at[p, :, pl.ds(0, 768)],
                    wd.at[shard_of(me, slot, False)],
                    sem_d.at[slot],
                )
            )
        start += each
    for copy in copies_a + copies_b + copies_d:
        copy.start()
    x = x_ref[...]

    def units(w, cols):
        gate = lax.dot_general(x, w[:, :width], NT, preferred_element_type=F32)
        upper = lax.dot_general(x, w[:, width:], NT, preferred_element_type=F32)
        hid[:, cols] = (gate / (1.0 + jnp.exp(-gate)) * upper).astype(BF16)

    for c in range(2):
        for copy in copies_a[4 * c : 4 * (c + 1)]:
            copy.wait()
        units(wa[16 * c : 16 * (c + 1)].reshape(256, 2 * width), slice(256 * c, 256 * (c + 1)))
    for copy in copies_b:
        copy.wait()
    units(wb[...].reshape(256, 2 * width), slice(512, 768))
    hidden = lax.dot_general(hid[...], order_ref[...], NN, preferred_element_type=F32).astype(BF16)
    for copy in copies_d:
        copy.wait()
    shards, feats, ff = wd.shape
    group = shards // sem_o.shape[0]
    copies_o = []
    for n in range(shards // group):
        down = wd[group * n : group * (n + 1)].reshape(group * feats, ff)
        cols = pl.ds(group * feats * n, group * feats)
        out_ref[:, cols] = lax.dot_general(
            hidden, down, NT, preferred_element_type=F32
        ).astype(BF16)
        copies_o.append(
            pltpu.make_async_copy(out_ref.at[:, cols], out_hbm.at[:, cols], sem_o.at[n])
        )
        copies_o[-1].start()
    for copy in copies_o:
        copy.wait()


def run_expert(x, order, pieces_a, pieces_b):
    rows, width = x.shape
    ff = order.shape[0]
    shards = 32
    return pl.pallas_call(
        expert_kernel,
        out_shape=jax.ShapeDtypeStruct((rows, width), BF16),
        in_specs=[VMEM, VMEM] + [ANY] * 12,
        out_specs=ANY,
        scratch_shapes=[
            pltpu.VMEM((rows, width), BF16),
            pltpu.VMEM((shards, 16, 2 * width), BF16),
            pltpu.VMEM((shards, 8, 2 * width), BF16),
            pltpu.VMEM((shards, width // shards, ff), BF16),
            pltpu.VMEM((rows, ff), BF16),
            pltpu.SemaphoreType.DMA((8,)),
            pltpu.SemaphoreType.DMA((48,)),
            pltpu.SemaphoreType.DMA((32,)),
            pltpu.SemaphoreType.DMA((4,)),
        ],
        compiler_params=pltpu.CompilerParams(vmem_limit_bytes=50 << 20),
        cost_estimate=pl.CostEstimate(
            flops=6 * rows * width * ff,
            bytes_accessed=6 * width * ff + 4 * x.size,
            transcendentals=rows * ff,
        ),
        name="expert",
    )(x, order, *pieces_a, *pieces_b)


def last_kernel(expert_ref, probs_ref, x_ref, out_ref, *, ring, cap):
    expert = expert_ref[...]
    count = expert.shape[0]
    member = lax.broadcasted_iota(jnp.int32, (count, ring), 1) == expert
    before = lax.broadcasted_iota(jnp.int32, (count, count), 1) < lax.broadcasted_iota(
        jnp.int32, (count, count), 0
    )
    earlier = lax.dot_general(
        before.astype(F32), member.astype(F32), NN, preferred_element_type=F32
    )
    slot = jnp.sum(jnp.where(member, earlier, 0.0), axis=1, keepdims=True).astype(jnp.int32)
    place = expert * cap + slot
    pick = lax.broadcasted_iota(jnp.int32, (count, ring * cap), 1) == place
    probs = probs_ref[...]
    share = probs[:, :1] / jnp.sum(probs, axis=1, keepdims=True)
    got = lax.dot_general(
        pick.astype(F32).astype(BF16), x_ref[...], NN, preferred_element_type=F32
    )
    out_ref[...] = (share * got).astype(BF16)


def exchange(x, ring):
    blocks = x.reshape(ring, x.shape[0] // ring, x.shape[1])
    return lax.all_to_all(blocks, "expert", split_axis=0, concat_axis=0, tiled=True).reshape(x.shape)


def local(tokens, norm_gain, route_probs, window_expert, w_gate_up, w_down):
    tok_count, width = tokens.shape
    ring = lax.axis_size("expert")
    cap = 3 * tok_count // ring
    rows = ring * cap
    ff = w_down.shape[2]
    sent, mine_a, mine_b = pl.pallas_call(
        functools.partial(prepare_kernel, ring=ring, cap=cap),
        out_shape=[
            jax.ShapeDtypeStruct((rows, width), BF16),
            jax.ShapeDtypeStruct((1, 16, 2 * width), BF16),
            jax.ShapeDtypeStruct((1, 64, 1280), BF16),
        ],
        in_specs=[ANY] * 5,
        out_specs=[ANY, VMEM, VMEM],
        scratch_shapes=[
            pltpu.VMEM((rows, width), BF16),
            pltpu.VMEM((tok_count, width), BF16),
            pltpu.VMEM((1, width), F32),
            pltpu.VMEM((1, tok_count), jnp.int32),
            pltpu.SemaphoreType.DMA((13,)),
            pltpu.SemaphoreType.DMA((3,)),
        ],
        compiler_params=pltpu.CompilerParams(vmem_limit_bytes=60 << 20),
        cost_estimate=pl.CostEstimate(
            flops=6 * tok_count * tok_count * width,
            bytes_accessed=8 * tokens.size,
            transcendentals=0,
        ),
        name="prepare",
    )(tokens, norm_gain[None, :], window_expert[None, :], w_gate_up[0], w_down[0])
    x = exchange(sent, ring)
    made = run_expert(x, hidden_order(ff), *gather(mine_a, mine_b))
    return pl.pallas_call(
        functools.partial(last_kernel, ring=ring, cap=cap),
        out_shape=jax.ShapeDtypeStruct((tok_count, width), BF16),
        in_specs=[VMEM] * 3,
        out_specs=VMEM,
        cost_estimate=pl.CostEstimate(
            flops=6 * tok_count * tok_count * width, bytes_accessed=8 * tokens.size, transcendentals=0
        ),
        compiler_params=pltpu.CompilerParams(vmem_limit_bytes=16 << 20),
        name="last",
    )(window_expert[:, None], route_probs, exchange(made, ring))


def solution(mesh):
    placed = (
        P(("dp", "expert"), None),
        P(),
        P(("dp", "expert"), None),
        P(("dp", "expert")),
        P("expert", "dp", None),
        P("expert", "dp", None),
    )
    return jax.shard_map(
        local, mesh=mesh, in_specs=placed, out_specs=P(("dp", "expert"), None), check_vma=False
    )
```

```python
import functools

import jax
import jax.numpy as jnp
import numpy as np
from jax import lax
from jax.experimental import pallas as pl
from jax.experimental.pallas import tpu as pltpu
from jax.sharding import PartitionSpec as P

F32, BF16 = jnp.float32, jnp.bfloat16
NT = (((1,), (1,)), ((), ()))
NN = (((1,), (0,)), ((), ()))
VMEM = pl.BlockSpec(memory_space=pltpu.VMEM)
HBM = pl.BlockSpec(memory_space=pltpu.HBM)
ANY = pl.BlockSpec(memory_space=pl.ANY)


def trade(x, where):
    return lax.ppermute(x, "dp", [(i, where(i)) for i in range(lax.axis_size("dp"))])


def flip(mask):
    return lambda i: i ^ mask


def turn(bit, hops):
    return lambda i: (i & ~(3 << bit)) | ((((i >> bit) + hops) & 3) << bit)


X_BIT, Y_BIT, CORE = 3, 1, 1
GRAY = (0, 1, 3, 2)
TURNS = (0, -1, 1, 2)


def gather(a, b):
    for step in (1, 3):
        a_in, b_in = lax.optimization_barrier(
            (trade(a, flip(step << X_BIT)), trade(b, flip(step << Y_BIT)))
        )
        a, b = jnp.concatenate([a, a_in], axis=0), jnp.concatenate([b, b_in], axis=0)
    a_l, b_l, a_r, b_r = lax.optimization_barrier(
        (
            trade(a, turn(Y_BIT, 1)),
            trade(b, turn(X_BIT, 1)),
            trade(a, turn(Y_BIT, -1)),
            trade(b, turn(X_BIT, -1)),
        )
    )
    a12, b12 = jnp.concatenate([a, a_l, a_r], axis=0), jnp.concatenate([b, b_l, b_r], axis=0)
    a_0, b_0, a_1, b_1 = (
        trade(a_l[:2], turn(Y_BIT, 1)),
        trade(b_l[:2], turn(X_BIT, 1)),
        trade(a_r[2:], turn(Y_BIT, -1)),
        trade(b_r[2:], turn(X_BIT, -1)),
    )
    a4, b4 = jnp.concatenate([a_0, a_1], axis=0), jnp.concatenate([b_0, b_1], axis=0)
    near = flip(CORE)
    return (a12, a4, trade(a12, near), trade(a4, near)), (b12, b4, trade(b12, near), trade(b4, near))


def shard_of(me, slot, x_first):
    x, y, core = me >> X_BIT, (me >> Y_BIT) & 3, me & 1
    group, k = (slot >> 2) & 3, slot & 3
    if x_first:
        x, y = x ^ GRAY[k], (y + TURNS[group]) & 3
    else:
        x, y = (x + TURNS[group]) & 3, y ^ GRAY[k]
    return (x << X_BIT) | (y << Y_BIT) | (core ^ (slot >> 4))


def hidden_order(ff):
    me = lax.axis_index("dp")
    k = np.arange(ff)
    x_first = k < 512
    slot = np.where(x_first, k >> 4, (k - 512) >> 3)
    low = np.where(x_first, k & 15, 16 + (k & 7))
    pair, ring = np.array(GRAY)[slot & 3], np.array(TURNS)[(slot >> 2) & 3]
    x = (((me >> X_BIT) ^ np.where(x_first, pair, 0)) + np.where(x_first, 0, ring)) & 3
    y = ((((me >> Y_BIT) & 3) ^ np.where(x_first, 0, pair)) + np.where(x_first, ring, 0)) & 3
    shard = (x << X_BIT) | (y << Y_BIT) | ((me & 1) ^ (slot >> 4))
    unit = (shard * 24 + low).astype(jnp.int32)
    return (unit[:, None] == jnp.arange(ff, dtype=jnp.int32)[None, :]).astype(BF16)


def prepare_kernel(*refs, ring, cap):
    tok_hbm, gain_hbm, expert_hbm, both_hbm, down_hbm = refs[:5]
    out_ref, a_ref, b_ref, tok_ref, gain_ref, expert_ref, sems = refs[5:]
    moves = [
        (tok_hbm, tok_ref),
        (gain_hbm, gain_ref),
        (expert_hbm, expert_ref),
        (both_hbm.at[pl.ds(0, 16)], a_ref.at[0]),
        (down_hbm, b_ref.at[0, :, pl.ds(0, 768)]),
    ] + [
        (both_hbm.at[pl.ds(16, 8), pl.ds(512 * j, 512)], b_ref.at[0, pl.ds(8 * j, 8), pl.ds(768, 512)])
        for j in range(8)
    ]
    copies = [pltpu.make_async_copy(*move, sems.at[i]) for i, move in enumerate(moves)]
    for copy in copies:
        copy.start()
    for copy in copies[:3]:
        copy.wait()
    values = tok_ref[...].astype(F32)
    meansq = jnp.mean(values * values, axis=1, keepdims=True)
    normed = (values * lax.rsqrt(meansq + 1e-06) * gain_ref[...]).astype(BF16)
    expert = expert_ref[...]
    count = expert.shape[1]
    member = lax.broadcasted_iota(jnp.int32, (ring, count), 0) == expert
    before = lax.broadcasted_iota(jnp.int32, (count, count), 0) < lax.broadcasted_iota(
        jnp.int32, (count, count), 1
    )
    earlier = lax.dot_general(
        member.astype(F32), before.astype(F32), NN, preferred_element_type=F32
    )
    slot = jnp.sum(jnp.where(member, earlier, 0.0), axis=0, keepdims=True).astype(jnp.int32)
    place = expert * cap + slot
    pick = lax.broadcasted_iota(jnp.int32, (ring * cap, count), 0) == place
    out_ref[...] = lax.dot_general(
        pick.astype(F32).astype(BF16), normed, NN, preferred_element_type=F32
    ).astype(BF16)
    for copy in copies[3:]:
        copy.wait()


def expert_kernel(x_hbm, order_ref, *rest):
    pieces_a, pieces_b = rest[:4], rest[4:8]
    out_hbm, x_ref, out_ref, wa, wb, wd, hid, sem_x, sem_a, sem_b, sem_d, sem_o = rest[8:]
    width = x_ref.shape[1]
    me = lax.axis_index("dp")
    copy_x = pltpu.make_async_copy(x_hbm, x_ref, sem_x)
    copies_a, copies_b, copies_d = [], [], []
    start = 0
    for q, (piece_a, piece_b) in enumerate(zip(pieces_a, pieces_b)):
        each = piece_a.shape[0]
        copies_a.append(
            pltpu.make_async_copy(piece_a, wa.at[pl.ds(start, each)], sem_a.at[q])
        )
        for j in range(8):
            copies_b.append(
                pltpu.make_async_copy(
                    piece_b.at[:, pl.ds(8 * j, 8), pl.ds(768, 512)],
                    wb.at[pl.ds(start, each), :, pl.ds(512 * j, 512)],
                    sem_b.at[8 * q + j],
                )
            )
        for p in range(each):
            slot = start + p
            copies_d.append(
                pltpu.make_async_copy(
                    piece_b.at[p, :, pl.ds(0, 768)],
                    wd.at[shard_of(me, slot, False)],
                    sem_d.at[slot],
                )
            )
        start += each
    for copy in [copy_x] + copies_a:
        copy.start()
    copy_x.wait()
    x = x_ref[...]

    def units(w, cols):
        gate = lax.dot_general(x, w[:, :width], NT, preferred_element_type=F32)
        upper = lax.dot_general(x, w[:, width:], NT, preferred_element_type=F32)
        hid[:, cols] = (gate / (1.0 + jnp.exp(-gate)) * upper).astype(BF16)

    for c in range(2):
        copies_a[2 * c].wait()
        copies_a[2 * c + 1].wait()
        for copy in (copies_b, copies_d)[c]:
            copy.start()
        units(wa[16 * c : 16 * (c + 1)].reshape(256, 2 * width), slice(256 * c, 256 * (c + 1)))
    for copy in copies_b:
        copy.wait()
    units(wb[...].reshape(256, 2 * width), slice(512, 768))
    hidden = lax.dot_general(hid[...], order_ref[...], NN, preferred_element_type=F32).astype(BF16)
    for copy in copies_d:
        copy.wait()
    shards, feats, ff = wd.shape
    group = shards // sem_o.shape[0]
    copies_o = []
    for n in range(shards // group):
        down = wd[group * n : group * (n + 1)].reshape(group * feats, ff)
        cols = pl.ds(group * feats * n, group * feats)
        out_ref[:, cols] = lax.dot_general(
            hidden, down, NT, preferred_element_type=F32
        ).astype(BF16)
        copies_o.append(
            pltpu.make_async_copy(out_ref.at[:, cols], out_hbm.at[:, cols], sem_o.at[n])
        )
        copies_o[-1].start()
    for copy in copies_o:
        copy.wait()


def run_expert(x, order, pieces_a, pieces_b):
    rows, width = x.shape
    ff = order.shape[0]
    shards = 32
    return pl.pallas_call(
        expert_kernel,
        out_shape=jax.ShapeDtypeStruct((rows, width), BF16),
        in_specs=[ANY, VMEM] + [ANY] * 8,
        out_specs=ANY,
        scratch_shapes=[
            pltpu.VMEM((rows, width), BF16),
            pltpu.VMEM((rows, width), BF16),
            pltpu.VMEM((shards, 16, 2 * width), BF16),
            pltpu.VMEM((shards, 8, 2 * width), BF16),
            pltpu.VMEM((shards, width // shards, ff), BF16),
            pltpu.VMEM((rows, ff), BF16),
            pltpu.SemaphoreType.DMA,
            pltpu.SemaphoreType.DMA((4,)),
            pltpu.SemaphoreType.DMA((32,)),
            pltpu.SemaphoreType.DMA((32,)),
            pltpu.SemaphoreType.DMA((4,)),
        ],
        compiler_params=pltpu.CompilerParams(vmem_limit_bytes=46 << 20),
        cost_estimate=pl.CostEstimate(
            flops=6 * rows * width * ff,
            bytes_accessed=6 * width * ff + 4 * x.size,
            transcendentals=rows * ff,
        ),
        name="expert",
    )(x, order, *pieces_a, *pieces_b)


def last_kernel(expert_ref, probs_ref, x_ref, out_ref, *, ring, cap):
    expert = expert_ref[...]
    count = expert.shape[0]
    member = lax.broadcasted_iota(jnp.int32, (count, ring), 1) == expert
    before = lax.broadcasted_iota(jnp.int32, (count, count), 1) < lax.broadcasted_iota(
        jnp.int32, (count, count), 0
    )
    earlier = lax.dot_general(
        before.astype(F32), member.astype(F32), NN, preferred_element_type=F32
    )
    slot = jnp.sum(jnp.where(member, earlier, 0.0), axis=1, keepdims=True).astype(jnp.int32)
    place = expert * cap + slot
    pick = lax.broadcasted_iota(jnp.int32, (count, ring * cap), 1) == place
    probs = probs_ref[...]
    share = probs[:, :1] / jnp.sum(probs, axis=1, keepdims=True)
    got = lax.dot_general(
        pick.astype(F32).astype(BF16), x_ref[...], NN, preferred_element_type=F32
    )
    out_ref[...] = (share * got).astype(BF16)


def exchange(x, ring):
    blocks = x.reshape(ring, x.shape[0] // ring, x.shape[1])
    return lax.all_to_all(blocks, "expert", split_axis=0, concat_axis=0, tiled=True).reshape(x.shape)


def local(tokens, norm_gain, route_probs, window_expert, w_gate_up, w_down):
    tok_count, width = tokens.shape
    ring = lax.axis_size("expert")
    cap = 3 * tok_count // ring
    rows = ring * cap
    ff = w_down.shape[2]
    sent, mine_a, mine_b = pl.pallas_call(
        functools.partial(prepare_kernel, ring=ring, cap=cap),
        out_shape=[
            jax.ShapeDtypeStruct((rows, width), BF16),
            jax.ShapeDtypeStruct((1, 16, 2 * width), BF16),
            jax.ShapeDtypeStruct((1, 64, 1280), BF16),
        ],
        in_specs=[ANY] * 5,
        out_specs=[VMEM] * 3,
        scratch_shapes=[
            pltpu.VMEM((tok_count, width), BF16),
            pltpu.VMEM((1, width), F32),
            pltpu.VMEM((1, tok_count), jnp.int32),
            pltpu.SemaphoreType.DMA((13,)),
        ],
        compiler_params=pltpu.CompilerParams(vmem_limit_bytes=60 << 20),
        cost_estimate=pl.CostEstimate(
            flops=6 * tok_count * tok_count * width,
            bytes_accessed=8 * tokens.size,
            transcendentals=0,
        ),
        name="prepare",
    )(tokens, norm_gain[None, :], window_expert[None, :], w_gate_up[0], w_down[0])
    x = exchange(sent, ring)
    made = run_expert(x, hidden_order(ff), *gather(mine_a, mine_b))
    return pl.pallas_call(
        functools.partial(last_kernel, ring=ring, cap=cap),
        out_shape=jax.ShapeDtypeStruct((tok_count, width), BF16),
        in_specs=[VMEM] * 3,
        out_specs=VMEM,
        cost_estimate=pl.CostEstimate(
            flops=6 * tok_count * tok_count * width, bytes_accessed=8 * tokens.size, transcendentals=0
        ),
        compiler_params=pltpu.CompilerParams(vmem_limit_bytes=16 << 20),
        name="last",
    )(window_expert[:, None], route_probs, exchange(made, ring))


def solution(mesh):
    placed = (
        P(("dp", "expert"), None),
        P(),
        P(("dp", "expert"), None),
        P(("dp", "expert")),
        P("expert", "dp", None),
        P("expert", "dp", None),
    )
    return jax.shard_map(
        local, mesh=mesh, in_specs=placed, out_specs=P(("dp", "expert"), None), check_vma=False
    )
```

```python
import functools

import jax
import jax.numpy as jnp
import numpy as np
from jax import lax
from jax.experimental import pallas as pl
from jax.experimental.pallas import tpu as pltpu
from jax.sharding import PartitionSpec as P

F32, BF16 = jnp.float32, jnp.bfloat16
NT = (((1,), (1,)), ((), ()))
NN = (((1,), (0,)), ((), ()))
VMEM = pl.BlockSpec(memory_space=pltpu.VMEM)
HBM = pl.BlockSpec(memory_space=pltpu.HBM)
ANY = pl.BlockSpec(memory_space=pl.ANY)


def trade(x, where):
    return lax.ppermute(x, "dp", [(i, where(i)) for i in range(lax.axis_size("dp"))])


def flip(mask):
    return lambda i: i ^ mask


def turn(bit, hops):
    return lambda i: (i & ~(3 << bit)) | ((((i >> bit) + hops) & 3) << bit)


X_BIT, Y_BIT, CORE = 3, 1, 1
GRAY = (0, 1, 3, 2)
TURNS = (0, -1, 1, 2)


def gather(a, b):
    for step in (1, 3):
        a_in, b_in = lax.optimization_barrier(
            (trade(a, flip(step << X_BIT)), trade(b, flip(step << Y_BIT)))
        )
        a, b = jnp.concatenate([a, a_in], axis=0), jnp.concatenate([b, b_in], axis=0)
    a_l, b_l, a_r, b_r = lax.optimization_barrier(
        (
            trade(a, turn(Y_BIT, 1)),
            trade(b, turn(X_BIT, 1)),
            trade(a, turn(Y_BIT, -1)),
            trade(b, turn(X_BIT, -1)),
        )
    )
    a12, b12 = jnp.concatenate([a, a_l, a_r], axis=0), jnp.concatenate([b, b_l, b_r], axis=0)
    a_0, b_0, a_1, b_1 = (
        trade(a_l[:2], turn(Y_BIT, 1)),
        trade(b_l[:2], turn(X_BIT, 1)),
        trade(a_r[2:], turn(Y_BIT, -1)),
        trade(b_r[2:], turn(X_BIT, -1)),
    )
    a4, b4 = jnp.concatenate([a_0, a_1], axis=0), jnp.concatenate([b_0, b_1], axis=0)
    near = flip(CORE)
    return (a12, a4, trade(a12, near), trade(a4, near)), (b12, b4, trade(b12, near), trade(b4, near))


def shard_of(me, slot, x_first):
    x, y, core = me >> X_BIT, (me >> Y_BIT) & 3, me & 1
    group, k = (slot >> 2) & 3, slot & 3
    if x_first:
        x, y = x ^ GRAY[k], (y + TURNS[group]) & 3
    else:
        x, y = (x + TURNS[group]) & 3, y ^ GRAY[k]
    return (x << X_BIT) | (y << Y_BIT) | (core ^ (slot >> 4))


def hidden_order(ff):
    me = lax.axis_index("dp")
    k = np.arange(ff)
    x_first = k < 512
    slot = np.where(x_first, k >> 4, (k - 512) >> 3)
    low = np.where(x_first, k & 15, 16 + (k & 7))
    pair, ring = np.array(GRAY)[slot & 3], np.array(TURNS)[(slot >> 2) & 3]
    x = (((me >> X_BIT) ^ np.where(x_first, pair, 0)) + np.where(x_first, 0, ring)) & 3
    y = ((((me >> Y_BIT) & 3) ^ np.where(x_first, 0, pair)) + np.where(x_first, ring, 0)) & 3
    shard = (x << X_BIT) | (y << Y_BIT) | ((me & 1) ^ (slot >> 4))
    unit = (shard * 24 + low).astype(jnp.int32)
    return (unit[:, None] == jnp.arange(ff, dtype=jnp.int32)[None, :]).astype(BF16)


def prepare_kernel(*refs, ring, cap):
    tok_hbm, gain_hbm, expert_hbm, both_hbm, down_hbm = refs[:5]
    out_ref, a_ref, b_ref, tok_ref, gain_ref, expert_ref, sems = refs[5:]
    moves = [
        (tok_hbm, tok_ref),
        (gain_hbm, gain_ref),
        (expert_hbm, expert_ref),
        (both_hbm.at[pl.ds(0, 16)], a_ref.at[0]),
        (down_hbm, b_ref.at[0, :, pl.ds(0, 768)]),
    ] + [
        (both_hbm.at[pl.ds(16, 8), pl.ds(512 * j, 512)], b_ref.at[0, pl.ds(8 * j, 8), pl.ds(768, 512)])
        for j in range(8)
    ]
    copies = [pltpu.make_async_copy(*move, sems.at[i]) for i, move in enumerate(moves)]
    for copy in copies:
        copy.start()
    for copy in copies[:3]:
        copy.wait()
    values = tok_ref[...].astype(F32)
    meansq = jnp.mean(values * values, axis=1, keepdims=True)
    normed = (values * lax.rsqrt(meansq + 1e-06) * gain_ref[...]).astype(BF16)
    expert = expert_ref[...]
    count = expert.shape[1]
    member = lax.broadcasted_iota(jnp.int32, (ring, count), 0) == expert
    before = lax.broadcasted_iota(jnp.int32, (count, count), 0) < lax.broadcasted_iota(
        jnp.int32, (count, count), 1
    )
    earlier = lax.dot_general(
        member.astype(F32), before.astype(F32), NN, preferred_element_type=F32
    )
    slot = jnp.sum(jnp.where(member, earlier, 0.0), axis=0, keepdims=True).astype(jnp.int32)
    place = expert * cap + slot
    pick = lax.broadcasted_iota(jnp.int32, (ring * cap, count), 0) == place
    out_ref[...] = lax.dot_general(
        pick.astype(F32).astype(BF16), normed, NN, preferred_element_type=F32
    ).astype(BF16)
    for copy in copies[3:]:
        copy.wait()


def expert_kernel(x_hbm, order_ref, *rest):
    pieces_a, pieces_b = rest[:4], rest[4:8]
    out_hbm, x_ref, out_ref, wa, wb, wd, hid, sem_x, sem_a, sem_b, sem_d, sem_o = rest[8:]
    width = x_ref.shape[1]
    me = lax.axis_index("dp")
    copy_x = pltpu.make_async_copy(x_hbm, x_ref, sem_x)
    copies_a, copies_b, copies_d = [], [], []
    start = 0
    for q, (piece_a, piece_b) in enumerate(zip(pieces_a, pieces_b)):
        each = piece_a.shape[0]
        copies_a.append(
            pltpu.make_async_copy(piece_a, wa.at[pl.ds(start, each)], sem_a.at[q])
        )
        for j in range(8):
            copies_b.append(
                pltpu.make_async_copy(
                    piece_b.at[:, pl.ds(8 * j, 8), pl.ds(768, 512)],
                    wb.at[pl.ds(start, each), :, pl.ds(512 * j, 512)],
                    sem_b.at[8 * q + j],
                )
            )
        for p in range(each):
            slot = start + p
            copies_d.append(
                pltpu.make_async_copy(
                    piece_b.at[p, :, pl.ds(0, 768)],
                    wd.at[shard_of(me, slot, False)],
                    sem_d.at[slot],
                )
            )
        start += each
    for copy in [copy_x] + copies_a + copies_b + copies_d:
        copy.start()
    copy_x.wait()
    x = x_ref[...]

    def products(w):
        gate = lax.dot_general(x, w[:, :width], NT, preferred_element_type=F32)
        upper = lax.dot_general(x, w[:, width:], NT, preferred_element_type=F32)
        return gate, upper

    def activate(c, gate, upper):
        hid[:, 256 * c : 256 * (c + 1)] = (gate / (1.0 + jnp.exp(-gate)) * upper).astype(BF16)

    copies_a[0].wait()
    copies_a[1].wait()
    first = products(wa[:16].reshape(256, 2 * width))
    copies_a[2].wait()
    copies_a[3].wait()
    second = products(wa[16:].reshape(256, 2 * width))
    activate(0, *first)
    for copy in copies_b:
        copy.wait()
    third = products(wb[...].reshape(256, 2 * width))
    activate(1, *second)
    activate(2, *third)
    hidden = lax.dot_general(hid[...], order_ref[...], NN, preferred_element_type=F32).astype(BF16)
    for copy in copies_d:
        copy.wait()
    shards, feats, ff = wd.shape
    group = shards // sem_o.shape[0]
    copies_o = []
    for n in range(shards // group):
        down = wd[group * n : group * (n + 1)].reshape(group * feats, ff)
        cols = pl.ds(group * feats * n, group * feats)
        out_ref[:, cols] = lax.dot_general(
            hidden, down, NT, preferred_element_type=F32
        ).astype(BF16)
        copies_o.append(
            pltpu.make_async_copy(out_ref.at[:, cols], out_hbm.at[:, cols], sem_o.at[n])
        )
        copies_o[-1].start()
    for copy in copies_o:
        copy.wait()


def run_expert(x, order, pieces_a, pieces_b):
    rows, width = x.shape
    ff = order.shape[0]
    shards = 32
    return pl.pallas_call(
        expert_kernel,
        out_shape=jax.ShapeDtypeStruct((rows, width), BF16),
        in_specs=[ANY, VMEM] + [ANY] * 8,
        out_specs=ANY,
        scratch_shapes=[
            pltpu.VMEM((rows, width), BF16),
            pltpu.VMEM((rows, width), BF16),
            pltpu.VMEM((shards, 16, 2 * width), BF16),
            pltpu.VMEM((shards, 8, 2 * width), BF16),
            pltpu.VMEM((shards, width // shards, ff), BF16),
            pltpu.VMEM((rows, ff), BF16),
            pltpu.SemaphoreType.DMA,
            pltpu.SemaphoreType.DMA((4,)),
            pltpu.SemaphoreType.DMA((32,)),
            pltpu.SemaphoreType.DMA((32,)),
            pltpu.SemaphoreType.DMA((4,)),
        ],
        compiler_params=pltpu.CompilerParams(vmem_limit_bytes=46 << 20),
        cost_estimate=pl.CostEstimate(
            flops=6 * rows * width * ff,
            bytes_accessed=6 * width * ff + 4 * x.size,
            transcendentals=rows * ff,
        ),
        name="expert",
    )(x, order, *pieces_a, *pieces_b)


def last_kernel(expert_ref, probs_ref, x_ref, out_ref, *, ring, cap):
    expert = expert_ref[...]
    count = expert.shape[0]
    member = lax.broadcasted_iota(jnp.int32, (count, ring), 1) == expert
    before = lax.broadcasted_iota(jnp.int32, (count, count), 1) < lax.broadcasted_iota(
        jnp.int32, (count, count), 0
    )
    earlier = lax.dot_general(
        before.astype(F32), member.astype(F32), NN, preferred_element_type=F32
    )
    slot = jnp.sum(jnp.where(member, earlier, 0.0), axis=1, keepdims=True).astype(jnp.int32)
    place = expert * cap + slot
    pick = lax.broadcasted_iota(jnp.int32, (count, ring * cap), 1) == place
    probs = probs_ref[...]
    share = probs[:, :1] / jnp.sum(probs, axis=1, keepdims=True)
    got = lax.dot_general(
        pick.astype(F32).astype(BF16), x_ref[...], NN, preferred_element_type=F32
    )
    out_ref[...] = (share * got).astype(BF16)


def exchange(x, ring):
    blocks = x.reshape(ring, x.shape[0] // ring, x.shape[1])
    return lax.all_to_all(blocks, "expert", split_axis=0, concat_axis=0, tiled=True).reshape(x.shape)


def local(tokens, norm_gain, route_probs, window_expert, w_gate_up, w_down):
    tok_count, width = tokens.shape
    ring = lax.axis_size("expert")
    cap = 3 * tok_count // ring
    rows = ring * cap
    ff = w_down.shape[2]
    sent, mine_a, mine_b = pl.pallas_call(
        functools.partial(prepare_kernel, ring=ring, cap=cap),
        out_shape=[
            jax.ShapeDtypeStruct((rows, width), BF16),
            jax.ShapeDtypeStruct((1, 16, 2 * width), BF16),
            jax.ShapeDtypeStruct((1, 64, 1280), BF16),
        ],
        in_specs=[ANY] * 5,
        out_specs=[VMEM] * 3,
        scratch_shapes=[
            pltpu.VMEM((tok_count, width), BF16),
            pltpu.VMEM((1, width), F32),
            pltpu.VMEM((1, tok_count), jnp.int32),
            pltpu.SemaphoreType.DMA((13,)),
        ],
        compiler_params=pltpu.CompilerParams(vmem_limit_bytes=60 << 20),
        cost_estimate=pl.CostEstimate(
            flops=6 * tok_count * tok_count * width,
            bytes_accessed=8 * tokens.size,
            transcendentals=0,
        ),
        name="prepare",
    )(tokens, norm_gain[None, :], window_expert[None, :], w_gate_up[0], w_down[0])
    x = exchange(sent, ring)
    made = run_expert(x, hidden_order(ff), *gather(mine_a, mine_b))
    return pl.pallas_call(
        functools.partial(last_kernel, ring=ring, cap=cap),
        out_shape=jax.ShapeDtypeStruct((tok_count, width), BF16),
        in_specs=[VMEM] * 3,
        out_specs=VMEM,
        cost_estimate=pl.CostEstimate(
            flops=6 * tok_count * tok_count * width, bytes_accessed=8 * tokens.size, transcendentals=0
        ),
        compiler_params=pltpu.CompilerParams(vmem_limit_bytes=16 << 20),
        name="last",
    )(window_expert[:, None], route_probs, exchange(made, ring))


def solution(mesh):
    placed = (
        P(("dp", "expert"), None),
        P(),
        P(("dp", "expert"), None),
        P(("dp", "expert")),
        P("expert", "dp", None),
        P("expert", "dp", None),
    )
    return jax.shard_map(
        local, mesh=mesh, in_specs=placed, out_specs=P(("dp", "expert"), None), check_vma=False
    )
```

```python
import functools

import jax
import jax.numpy as jnp
import numpy as np
from jax import lax
from jax.experimental import pallas as pl
from jax.experimental.pallas import tpu as pltpu
from jax.sharding import PartitionSpec as P

F32, BF16 = jnp.float32, jnp.bfloat16
NT = (((1,), (1,)), ((), ()))
NN = (((1,), (0,)), ((), ()))
VMEM = pl.BlockSpec(memory_space=pltpu.VMEM)
HBM = pl.BlockSpec(memory_space=pltpu.HBM)
ANY = pl.BlockSpec(memory_space=pl.ANY)


def trade(x, where):
    return lax.ppermute(x, "dp", [(i, where(i)) for i in range(lax.axis_size("dp"))])


def flip(mask):
    return lambda i: i ^ mask


def turn(bit, hops):
    return lambda i: (i & ~(3 << bit)) | ((((i >> bit) + hops) & 3) << bit)


X_BIT, Y_BIT, CORE = 3, 1, 1
GRAY = (0, 1, 3, 2)
TURNS = (0, -1, 1, 2)


def gather(a, b):
    for step in (1, 3):
        a_in, b_in = lax.optimization_barrier(
            (trade(a, flip(step << X_BIT)), trade(b, flip(step << Y_BIT)))
        )
        a, b = jnp.concatenate([a, a_in], axis=0), jnp.concatenate([b, b_in], axis=0)
    a_l, b_l, a_r, b_r = lax.optimization_barrier(
        (
            trade(a, turn(Y_BIT, 1)),
            trade(b, turn(X_BIT, 1)),
            trade(a, turn(Y_BIT, -1)),
            trade(b, turn(X_BIT, -1)),
        )
    )
    a12, b12 = jnp.concatenate([a, a_l, a_r], axis=0), jnp.concatenate([b, b_l, b_r], axis=0)
    a_0, b_0, a_1, b_1 = (
        trade(a_l[:2], turn(Y_BIT, 1)),
        trade(b_l[:2], turn(X_BIT, 1)),
        trade(a_r[2:], turn(Y_BIT, -1)),
        trade(b_r[2:], turn(X_BIT, -1)),
    )
    near = flip(CORE)
    a_0, b_0, a_1, b_1, a_near, b_near = lax.optimization_barrier(
        (a_0, b_0, a_1, b_1, trade(a12, near), trade(b12, near))
    )
    a4, b4 = jnp.concatenate([a_0, a_1], axis=0), jnp.concatenate([b_0, b_1], axis=0)
    return (a12, a4, a_near, trade(a4, near)), (b12, b4, b_near, trade(b4, near))


def shard_of(me, slot, x_first):
    x, y, core = me >> X_BIT, (me >> Y_BIT) & 3, me & 1
    group, k = (slot >> 2) & 3, slot & 3
    if x_first:
        x, y = x ^ GRAY[k], (y + TURNS[group]) & 3
    else:
        x, y = (x + TURNS[group]) & 3, y ^ GRAY[k]
    return (x << X_BIT) | (y << Y_BIT) | (core ^ (slot >> 4))


def hidden_order(ff):
    me = lax.axis_index("dp")
    k = np.arange(ff)
    x_first = k < 512
    slot = np.where(x_first, k >> 4, (k - 512) >> 3)
    low = np.where(x_first, k & 15, 16 + (k & 7))
    pair, ring = np.array(GRAY)[slot & 3], np.array(TURNS)[(slot >> 2) & 3]
    x = (((me >> X_BIT) ^ np.where(x_first, pair, 0)) + np.where(x_first, 0, ring)) & 3
    y = ((((me >> Y_BIT) & 3) ^ np.where(x_first, 0, pair)) + np.where(x_first, ring, 0)) & 3
    shard = (x << X_BIT) | (y << Y_BIT) | ((me & 1) ^ (slot >> 4))
    unit = (shard * 24 + low).astype(jnp.int32)
    return (unit[:, None] == jnp.arange(ff, dtype=jnp.int32)[None, :]).astype(BF16)


def prepare_kernel(*refs, ring, cap):
    tok_hbm, gain_hbm, expert_hbm, both_hbm, down_hbm = refs[:5]
    out_ref, a_ref, b_ref, tok_ref, gain_ref, expert_ref, sems = refs[5:]
    moves = [
        (tok_hbm, tok_ref),
        (gain_hbm, gain_ref),
        (expert_hbm, expert_ref),
        (both_hbm.at[pl.ds(0, 16)], a_ref.at[0]),
        (down_hbm, b_ref.at[0, :, pl.ds(0, 768)]),
    ] + [
        (both_hbm.at[pl.ds(16, 8), pl.ds(512 * j, 512)], b_ref.at[0, pl.ds(8 * j, 8), pl.ds(768, 512)])
        for j in range(8)
    ]
    copies = [pltpu.make_async_copy(*move, sems.at[i]) for i, move in enumerate(moves)]
    for copy in copies:
        copy.start()
    for copy in copies[:3]:
        copy.wait()
    values = tok_ref[...].astype(F32)
    meansq = jnp.mean(values * values, axis=1, keepdims=True)
    normed = (values * lax.rsqrt(meansq + 1e-06) * gain_ref[...]).astype(BF16)
    expert = expert_ref[...]
    count = expert.shape[1]
    member = lax.broadcasted_iota(jnp.int32, (ring, count), 0) == expert
    before = lax.broadcasted_iota(jnp.int32, (count, count), 0) < lax.broadcasted_iota(
        jnp.int32, (count, count), 1
    )
    earlier = lax.dot_general(
        member.astype(F32), before.astype(F32), NN, preferred_element_type=F32
    )
    slot = jnp.sum(jnp.where(member, earlier, 0.0), axis=0, keepdims=True).astype(jnp.int32)
    place = expert * cap + slot
    pick = lax.broadcasted_iota(jnp.int32, (ring * cap, count), 0) == place
    out_ref[...] = lax.dot_general(
        pick.astype(F32).astype(BF16), normed, NN, preferred_element_type=F32
    ).astype(BF16)
    for copy in copies[3:]:
        copy.wait()


def expert_kernel(x_hbm, order_ref, *rest):
    pieces_a, pieces_b = rest[:4], rest[4:8]
    out_hbm, x_ref, out_ref, wa, wb, wd, hid, sem_x, sem_a, sem_b, sem_d, sem_o = rest[8:]
    width = x_ref.shape[1]
    me = lax.axis_index("dp")
    copy_x = pltpu.make_async_copy(x_hbm, x_ref, sem_x)
    copies_a, copies_b, copies_d = [], [], []
    start = 0
    for q, (piece_a, piece_b) in enumerate(zip(pieces_a, pieces_b)):
        each = piece_a.shape[0]
        copies_a.append(
            pltpu.make_async_copy(piece_a, wa.at[pl.ds(start, each)], sem_a.at[q])
        )
        for j in range(8):
            copies_b.append(
                pltpu.make_async_copy(
                    piece_b.at[:, pl.ds(8 * j, 8), pl.ds(768, 512)],
                    wb.at[pl.ds(start, each), :, pl.ds(512 * j, 512)],
                    sem_b.at[8 * q + j],
                )
            )
        for p in range(each):
            slot = start + p
            copies_d.append(
                pltpu.make_async_copy(
                    piece_b.at[p, :, pl.ds(0, 768)],
                    wd.at[shard_of(me, slot, False)],
                    sem_d.at[slot],
                )
            )
        start += each
    for copy in [copy_x] + copies_a + copies_b + copies_d:
        copy.start()
    copy_x.wait()
    x = x_ref[...]

    def units(w, cols):
        gate = lax.dot_general(x, w[:, :width], NT, preferred_element_type=F32)
        upper = lax.dot_general(x, w[:, width:], NT, preferred_element_type=F32)
        hid[:, cols] = (gate / (1.0 + jnp.exp(-gate)) * upper).astype(BF16)

    for c in range(2):
        copies_a[2 * c].wait()
        copies_a[2 * c + 1].wait()
        units(wa[16 * c : 16 * (c + 1)].reshape(256, 2 * width), slice(256 * c, 256 * (c + 1)))
    for copy in copies_b:
        copy.wait()
    units(wb[...].reshape(256, 2 * width), slice(512, 768))
    hidden = lax.dot_general(hid[...], order_ref[...], NN, preferred_element_type=F32).astype(BF16)
    for copy in copies_d:
        copy.wait()
    shards, feats, ff = wd.shape
    group = shards // sem_o.shape[0]
    copies_o = []
    for n in range(shards // group):
        down = wd[group * n : group * (n + 1)].reshape(group * feats, ff)
        cols = pl.ds(group * feats * n, group * feats)
        out_ref[:, cols] = lax.dot_general(
            hidden, down, NT, preferred_element_type=F32
        ).astype(BF16)
        copies_o.append(
            pltpu.make_async_copy(out_ref.at[:, cols], out_hbm.at[:, cols], sem_o.at[n])
        )
        copies_o[-1].start()
    for copy in copies_o:
        copy.wait()


def run_expert(x, order, pieces_a, pieces_b):
    rows, width = x.shape
    ff = order.shape[0]
    shards = 32
    return pl.pallas_call(
        expert_kernel,
        out_shape=jax.ShapeDtypeStruct((rows, width), BF16),
        in_specs=[ANY, VMEM] + [ANY] * 8,
        out_specs=ANY,
        scratch_shapes=[
            pltpu.VMEM((rows, width), BF16),
            pltpu.VMEM((rows, width), BF16),
            pltpu.VMEM((shards, 16, 2 * width), BF16),
            pltpu.VMEM((shards, 8, 2 * width), BF16),
            pltpu.VMEM((shards, width // shards, ff), BF16),
            pltpu.VMEM((rows, ff), BF16),
            pltpu.SemaphoreType.DMA,
            pltpu.SemaphoreType.DMA((4,)),
            pltpu.SemaphoreType.DMA((32,)),
            pltpu.SemaphoreType.DMA((32,)),
            pltpu.SemaphoreType.DMA((4,)),
        ],
        compiler_params=pltpu.CompilerParams(vmem_limit_bytes=50 << 20),
        cost_estimate=pl.CostEstimate(
            flops=6 * rows * width * ff,
            bytes_accessed=6 * width * ff + 4 * x.size,
            transcendentals=rows * ff,
        ),
        name="expert",
    )(x, order, *pieces_a, *pieces_b)


def last_kernel(expert_ref, probs_ref, x_ref, out_ref, *, ring, cap):
    expert = expert_ref[...]
    count = expert.shape[0]
    member = lax.broadcasted_iota(jnp.int32, (count, ring), 1) == expert
    before = lax.broadcasted_iota(jnp.int32, (count, count), 1) < lax.broadcasted_iota(
        jnp.int32, (count, count), 0
    )
    earlier = lax.dot_general(
        before.astype(F32), member.astype(F32), NN, preferred_element_type=F32
    )
    slot = jnp.sum(jnp.where(member, earlier, 0.0), axis=1, keepdims=True).astype(jnp.int32)
    place = expert * cap + slot
    pick = lax.broadcasted_iota(jnp.int32, (count, ring * cap), 1) == place
    probs = probs_ref[...]
    share = probs[:, :1] / jnp.sum(probs, axis=1, keepdims=True)
    got = lax.dot_general(
        pick.astype(F32).astype(BF16), x_ref[...], NN, preferred_element_type=F32
    )
    out_ref[...] = (share * got).astype(BF16)


def exchange(x, ring):
    blocks = x.reshape(ring, x.shape[0] // ring, x.shape[1])
    return lax.all_to_all(blocks, "expert", split_axis=0, concat_axis=0, tiled=True).reshape(x.shape)


def local(tokens, norm_gain, route_probs, window_expert, w_gate_up, w_down):
    tok_count, width = tokens.shape
    ring = lax.axis_size("expert")
    cap = 3 * tok_count // ring
    rows = ring * cap
    ff = w_down.shape[2]
    sent, mine_a, mine_b = pl.pallas_call(
        functools.partial(prepare_kernel, ring=ring, cap=cap),
        out_shape=[
            jax.ShapeDtypeStruct((rows, width), BF16),
            jax.ShapeDtypeStruct((1, 16, 2 * width), BF16),
            jax.ShapeDtypeStruct((1, 64, 1280), BF16),
        ],
        in_specs=[ANY] * 5,
        out_specs=[VMEM] * 3,
        scratch_shapes=[
            pltpu.VMEM((tok_count, width), BF16),
            pltpu.VMEM((1, width), F32),
            pltpu.VMEM((1, tok_count), jnp.int32),
            pltpu.SemaphoreType.DMA((13,)),
        ],
        compiler_params=pltpu.CompilerParams(vmem_limit_bytes=60 << 20),
        cost_estimate=pl.CostEstimate(
            flops=6 * tok_count * tok_count * width,
            bytes_accessed=8 * tokens.size,
            transcendentals=0,
        ),
        name="prepare",
    )(tokens, norm_gain[None, :], window_expert[None, :], w_gate_up[0], w_down[0])
    x = exchange(sent, ring)
    made = run_expert(x, hidden_order(ff), *gather(mine_a, mine_b))
    return pl.pallas_call(
        functools.partial(last_kernel, ring=ring, cap=cap),
        out_shape=jax.ShapeDtypeStruct((tok_count, width), BF16),
        in_specs=[VMEM] * 3,
        out_specs=VMEM,
        cost_estimate=pl.CostEstimate(
            flops=6 * tok_count * tok_count * width, bytes_accessed=8 * tokens.size, transcendentals=0
        ),
        compiler_params=pltpu.CompilerParams(vmem_limit_bytes=16 << 20),
        name="last",
    )(window_expert[:, None], route_probs, exchange(made, ring))


def solution(mesh):
    placed = (
        P(("dp", "expert"), None),
        P(),
        P(("dp", "expert"), None),
        P(("dp", "expert")),
        P("expert", "dp", None),
        P("expert", "dp", None),
    )
    return jax.shard_map(
        local, mesh=mesh, in_specs=placed, out_specs=P(("dp", "expert"), None), check_vma=False
    )
```
